32 devices in a mesh: cand: 4 (over x, core), seq: 8 (over z, y).
Axes of the slice: x: 2, y: 2, z: 4, core: 2. Of those that a mesh axis runs over, the one named last changes fastest.
Arguments:
- latent: bfloat16 [4, 384, 3072], P('cand', 'seq'), may hold values from -0.59765625 to 0.59765625
- timesteps: int32 [4], replicated, may hold values from 0 to 999
- positions: int32 [3, 384], replicated, may hold values from 0 to 63
- mod_weight: bfloat16 [3072, 9216], P('cand', 'seq'), may hold values from -0.109375 to 0.109375
- input_weight: bfloat16 [3072, 16, 384], P('cand', 'seq'), may hold values from -0.109375 to 0.109375
- output_weight: bfloat16 [16, 128, 3072], P('seq', None, 'cand'), may hold values from -0.75 to 0.75
- cotangent: bfloat16 [4, 384, 3072], P('cand', 'seq'), may hold values from -6 to 6
Outputs:
- block_out: bfloat16 [4, 384, 3072], P('cand', 'seq')
- latent_grad: float32 [4, 384, 3072], P('cand', 'seq')
The draws below stay inside these ranges and needn't reach their ends.
All inputs are finite; a program needn't handle non-finite values.
Results may differ from the reference program's by a relative error of at most 0.033.
Values may be sent and summed in bfloat16 or wider, within the bound.
A program may use at most 128 MiB of HBM per device.

```python
import jax
import jax.numpy as jnp
import numpy as np
from jax import lax

D = 3072
HEADS = 16
HEAD = 128
LEN = 384
CANDS = 4
GROUP = 2
ATT_WIDTH = 2048
N_SEQ = 8


def with_ends(drawn, stream_key, low, top_value):
    extent = drawn.shape
    place = [jax.random.randint(jax.random.fold_in(stream_key, axis), (), 0, extent[axis]) for axis in range(len(extent))]
    drawn = drawn.at[tuple(place)].set(low)
    longest = extent.index(max(extent))
    place[longest] = (place[longest] + 1) % extent[longest]
    return drawn.at[tuple(place)].set(top_value)


def levels(rng, shape, shards, low, largest):
    def one(axis_at, blocks):
        steps = jax.random.uniform(jax.random.fold_in(jax.random.fold_in(rng, 6), axis_at), (blocks,), jnp.float32, low / len(shards), largest / len(shards))
        return jnp.repeat(jnp.exp(steps), shape[axis_at] // blocks).reshape((-1,) + (1,) * (len(shape) - axis_at - 1))

    loudness = one(*shards[0])
    for cut in shards[1:]:
        loudness = loudness * one(*cut)
    return loudness


def scatter_about(key, extent, spread, bound, cuts=(), kind=jnp.bfloat16):
    loudness = levels(key, extent, cuts, -0.22, 0.18) if cuts else 1.0
    entries = jax.random.normal(key, extent, jnp.float32) * spread * loudness
    return jnp.minimum(jnp.maximum(entries, -bound), bound).astype(kind)


def setup_inputs(seed: int = 0) -> dict:
    arg_keys = jax.random.split(jax.random.key(seed), 8)
    return {
        "latent": scatter_about(arg_keys[0], (CANDS, LEN, D), 0.1, 0.59765625, ((0, 4), (1, 8))),
        "timesteps": with_ends(jax.random.randint(arg_keys[1], (CANDS,), 0, 1000), jax.random.fold_in(arg_keys[1], 1), 0, 999).astype(jnp.int32),
        "positions": with_ends(jax.random.randint(arg_keys[2], (3, LEN), 0, 64), jax.random.fold_in(arg_keys[2], 1), 0, 63).astype(jnp.int32),
        "mod_weight": scatter_about(arg_keys[3], (D, 3 * D), D ** -0.5, 0.109375, ((0, 4), (1, 8))),
        "input_weight": scatter_about(arg_keys[4], (D, HEADS, 3 * HEAD), D ** -0.5, 0.109375, ((0, 4), (1, 8))),
        "output_weight": scatter_about(arg_keys[5], (HEADS, HEAD, D), (ATT_WIDTH // 32) ** -0.5, 0.75, ((0, 8), (2, 4))),
        "cotangent": scatter_about(arg_keys[6], (CANDS, LEN, D), 1.0, 6.0, ((0, 4), (1, 8))),
    }


epsilon = 1e-06

def time_embed(timesteps, feature_width):
    half_size = feature_width // 2
    freq_rate = jnp.exp(-jnp.log(10000.0) * jnp.arange(half_size, dtype=jnp.float32) / half_size)
    angles = timesteps.astype(jnp.float32)[:, None] * freq_rate[None, :]
    return jnp.concatenate([jnp.cos(angles), jnp.sin(angles)], axis=1)

def rope_tables(positions, head_size):
    first_size = head_size // 8
    other_size = (head_size - first_size) // 2
    pieces = []
    swapped = []
    sign_vec = []
    offset = 0
    for axis_id, width_part in enumerate((first_size, other_size, other_size)):
        half_size = width_part // 2
        freq_rate = jnp.exp(-jnp.log(256.0) * 2.0 * jnp.arange(half_size, dtype=jnp.float32) / width_part)
        angle_part = positions[axis_id].astype(jnp.float32)[:, None] * freq_rate[None, :]
        pieces.append(angle_part)
        pieces.append(angle_part)
        swapped += list(range(offset + half_size, offset + width_part)) + list(range(offset, offset + half_size))
        sign_vec += [-1.0] * half_size + [1.0] * half_size
        offset += width_part
    angles = jnp.concatenate(pieces, axis=1)
    return (jnp.cos(angles), jnp.sin(angles), np.array(swapped, np.int32), np.array(sign_vec, np.float32))

def rotate(values, tables):
    cos_tab, sin_tab, swapped, sign_vec = tables
    return values * cos_tab + values[..., swapped] * sign_vec * sin_tab

def unrotate(values, tables):
    cos_tab, sin_tab, swapped, sign_vec = tables
    return values * cos_tab - (values * sin_tab)[..., swapped] * sign_vec

def rms_norm(values):
    inverse = lax.rsqrt(lax.optimization_barrier(jnp.mean(values * values, -1, keepdims=True)) + epsilon)
    return (values * inverse, inverse)

def rms_back(d_normed, normed, inverse):
    return inverse * (d_normed - normed * lax.optimization_barrier(jnp.mean(d_normed * normed, -1, keepdims=True)))

def layer_norm(values):
    centred = values - lax.optimization_barrier(jnp.mean(values, -1, keepdims=True))
    inverse_std = lax.rsqrt(lax.optimization_barrier(jnp.mean(centred * centred, -1, keepdims=True)) + epsilon)
    return (centred * inverse_std, inverse_std)

def layer_norm_back(d_normed, normed, inverse_std):
    return inverse_std * (d_normed - lax.optimization_barrier(jnp.mean(d_normed, -1, keepdims=True)) - normed * lax.optimization_barrier(jnp.mean(d_normed * normed, -1, keepdims=True)))

def attend(projected, tables):
    length, groups, triple = projected.shape
    head_size = triple // 3
    grouped = jnp.transpose(projected.reshape(length, groups, 3, head_size), (2, 1, 0, 3))
    query_n, query_inv = rms_norm(grouped[0])
    key_n, key_inv = rms_norm(grouped[1])
    q_rot = rotate(query_n, tables).astype(jnp.bfloat16)
    k_rot = rotate(key_n, tables).astype(jnp.bfloat16)
    values = grouped[2].astype(jnp.bfloat16)
    score_scale = head_size ** (-0.5)
    scores = jnp.einsum('gld,gmd->glm', q_rot.astype(jnp.float32), k_rot.astype(jnp.float32)) * score_scale
    weights = jnp.exp(scores - head_size ** 0.5)
    probs = weights / lax.optimization_barrier(jnp.sum(weights, -1, keepdims=True))
    probs_low = probs.astype(jnp.bfloat16)
    heads_out = jnp.einsum('glm,gmd->gld', probs_low.astype(jnp.float32), values.astype(jnp.float32))
    attended = jnp.transpose(heads_out, (1, 0, 2)).reshape(length, groups * head_size).astype(jnp.bfloat16)
    saved = (q_rot, k_rot, values, probs, probs_low, query_n, query_inv, key_n, key_inv)
    return (attended, saved)

def attend_back(d_attended, saved, tables):
    q_rot, k_rot, values, probs, probs_low, query_n, query_inv, key_n, key_inv = saved
    groups, length, head_size = q_rot.shape
    score_scale = head_size ** (-0.5)
    d_heads = jnp.transpose(d_attended.reshape(length, groups, head_size), (1, 0, 2)).astype(jnp.float32)
    d_values = jnp.einsum('glm,gld->gmd', probs_low.astype(jnp.float32), d_heads)
    d_probs = jnp.einsum('gld,gmd->glm', d_heads, values.astype(jnp.float32))
    d_scores = (probs * (d_probs - lax.optimization_barrier(jnp.sum(probs * d_probs, -1, keepdims=True)))).astype(jnp.bfloat16)
    d_qrot = jnp.einsum('glm,gmd->gld', d_scores.astype(jnp.float32), k_rot.astype(jnp.float32)) * score_scale
    d_krot = jnp.einsum('glm,gld->gmd', d_scores.astype(jnp.float32), q_rot.astype(jnp.float32)) * score_scale
    d_query = rms_back(unrotate(d_qrot, tables), query_n, query_inv)
    d_key = rms_back(unrotate(d_krot, tables), key_n, key_inv)
    stacked = jnp.stack([d_query, d_key, d_values], 0)
    return jnp.transpose(stacked, (2, 1, 0, 3)).reshape(length, groups * 3 * head_size).astype(jnp.bfloat16)

def reference(latent, timesteps, positions, mod_weight, input_weight, output_weight, cotangent):
    time_act = jax.nn.silu(time_embed(timesteps, D)).astype(jnp.bfloat16)
    modulation = jnp.dot(time_act, mod_weight, preferred_element_type=jnp.float32)
    tables = rope_tables(positions, HEAD)
    flat_in = input_weight.reshape(D, HEADS * 3 * HEAD)
    flat_out = output_weight.reshape(HEADS * HEAD, D)
    group_in = jnp.transpose(input_weight.reshape(D, N_SEQ, GROUP * 3 * HEAD), (1, 0, 2))

    def one_candidate(items):
        latent_one, mod_one, cot_one = items
        shift_vec = mod_one[:D]
        scale_vec = mod_one[D:2 * D]
        gate_vec = mod_one[2 * D:]
        normed, inverse_std = layer_norm(latent_one.astype(jnp.float32))
        modulated = (normed * (1.0 + scale_vec) + shift_vec).astype(jnp.bfloat16)
        projected = jnp.dot(modulated, flat_in, preferred_element_type=jnp.float32)
        attended, saved = attend(projected.reshape(LEN, HEADS, 3 * HEAD), tables)
        mixed = jnp.dot(attended, flat_out, preferred_element_type=jnp.float32)
        block_one = (latent_one.astype(jnp.float32) + gate_vec * mixed).astype(jnp.bfloat16)
        d_mixed = (cot_one.astype(jnp.float32) * gate_vec).astype(jnp.bfloat16)
        d_attended = lax.dot_general(d_mixed, flat_out, (((1,), (1,)), ((), ())), preferred_element_type=jnp.float32).astype(jnp.bfloat16)
        d_projected = attend_back(d_attended, saved, tables)
        d_groups = jnp.transpose(d_projected.reshape(LEN, N_SEQ, GROUP * 3 * HEAD), (1, 0, 2))

        def add_group(total, pieces):
            d_part, w_part = pieces
            partial_sum = lax.dot_general(d_part, w_part, (((1,), (1,)), ((), ())), preferred_element_type=jnp.float32)
            rounded = lax.optimization_barrier(partial_sum.astype(jnp.bfloat16))
            return (total + rounded.astype(jnp.float32), None)
        d_modulated, _unused = lax.scan(add_group, jnp.zeros((LEN, D), jnp.float32), (d_groups, group_in))
        grad_one = cot_one.astype(jnp.float32) + layer_norm_back(d_modulated * (1.0 + scale_vec), normed, inverse_std)
        return (block_one, grad_one)
    block_out, latent_grad = lax.map(one_candidate, (latent, modulation, cotangent))
    return (block_out, latent_grad)
```

```python
import jax
import jax.numpy as jnp
import numpy as np
from jax import lax
from jax.sharding import PartitionSpec as P

HEAD = 128


epsilon = 1e-06


def time_embed(timesteps, feature_width):
    half_size = feature_width // 2
    freq_rate = jnp.exp(-jnp.log(10000.0) * jnp.arange(half_size, dtype=jnp.float32) / half_size)
    angles = timesteps.astype(jnp.float32)[:, None] * freq_rate[None, :]
    return jnp.concatenate([jnp.cos(angles), jnp.sin(angles)], axis=1)


def rope_tables(positions, head_size):
    first_size = head_size // 8
    other_size = (head_size - first_size) // 2
    pieces = []
    swapped = []
    sign_vec = []
    offset = 0
    for axis_id, width_part in enumerate((first_size, other_size, other_size)):
        half_size = width_part // 2
        freq_rate = jnp.exp(
            -jnp.log(256.0) * 2.0 * jnp.arange(half_size, dtype=jnp.float32) / width_part
        )
        angle_part = positions[axis_id].astype(jnp.float32)[:, None] * freq_rate[None, :]
        pieces.append(angle_part)
        pieces.append(angle_part)
        swapped += list(range(offset + half_size, offset + width_part)) + list(
            range(offset, offset + half_size)
        )
        sign_vec += [-1.0] * half_size + [1.0] * half_size
        offset += width_part
    angles = jnp.concatenate(pieces, axis=1)
    return (
        jnp.cos(angles),
        jnp.sin(angles),
        np.array(swapped, np.int32),
        np.array(sign_vec, np.float32),
    )


def rotate(values, tables):
    cos_tab, sin_tab, swapped, sign_vec = tables
    return values * cos_tab + values[..., swapped] * sign_vec * sin_tab


def unrotate(values, tables):
    cos_tab, sin_tab, swapped, sign_vec = tables
    return values * cos_tab - (values * sin_tab)[..., swapped] * sign_vec


def rms_norm(values):
    inverse = lax.rsqrt(jnp.mean(values * values, -1, keepdims=True) + epsilon)
    return (values * inverse, inverse)


def rms_back(d_normed, normed, inverse):
    return inverse * (d_normed - normed * jnp.mean(d_normed * normed, -1, keepdims=True))


def layer_norm(values):
    centred = values - jnp.mean(values, -1, keepdims=True)
    inverse_std = lax.rsqrt(jnp.mean(centred * centred, -1, keepdims=True) + epsilon)
    return (centred * inverse_std, inverse_std)


def layer_norm_back(d_normed, normed, inverse_std):
    return inverse_std * (
        d_normed
        - jnp.mean(d_normed, -1, keepdims=True)
        - normed * jnp.mean(d_normed * normed, -1, keepdims=True)
    )


def times_transposed(left, right):
    return lax.dot_general(
        left, right, (((1,), (1,)), ((), ())), preferred_element_type=jnp.float32
    )


def attend(projected, tables):
    length, groups, triple = projected.shape
    head_size = triple // 3
    grouped = jnp.transpose(projected.reshape(length, groups, 3, head_size), (2, 1, 0, 3))
    query_n, query_inv = rms_norm(grouped[0])
    key_n, key_inv = rms_norm(grouped[1])
    q_rot = rotate(query_n, tables).astype(jnp.bfloat16)
    k_rot = rotate(key_n, tables).astype(jnp.bfloat16)
    values = grouped[2].astype(jnp.bfloat16)
    score_scale = head_size ** (-0.5)
    scores = (
        jnp.einsum("gld,gmd->glm", q_rot, k_rot, preferred_element_type=jnp.float32) * score_scale
    )
    weights = jnp.exp(scores - head_size**0.5)
    probs = weights / jnp.sum(weights, -1, keepdims=True)
    probs_low = probs.astype(jnp.bfloat16)
    heads_out = jnp.einsum("glm,gmd->gld", probs_low, values, preferred_element_type=jnp.float32)
    attended = (
        jnp.transpose(heads_out, (1, 0, 2)).reshape(length, groups * head_size).astype(jnp.bfloat16)
    )
    saved = (q_rot, k_rot, values, probs, probs_low, query_n, query_inv, key_n, key_inv)
    return (attended, saved)


def attend_back(d_attended, saved, tables):
    q_rot, k_rot, values, probs, probs_low, query_n, query_inv, key_n, key_inv = saved
    groups, length, head_size = q_rot.shape
    score_scale = head_size ** (-0.5)
    d_heads = jnp.transpose(d_attended.reshape(length, groups, head_size), (1, 0, 2))
    d_values = jnp.einsum("glm,gld->gmd", probs_low, d_heads, preferred_element_type=jnp.float32)
    d_probs = jnp.einsum("gld,gmd->glm", d_heads, values, preferred_element_type=jnp.float32)
    d_scores = (probs * (d_probs - jnp.sum(probs * d_probs, -1, keepdims=True))).astype(
        jnp.bfloat16
    )
    d_qrot = (
        jnp.einsum("glm,gmd->gld", d_scores, k_rot, preferred_element_type=jnp.float32)
        * score_scale
    )
    d_krot = (
        jnp.einsum("glm,gld->gmd", d_scores, q_rot, preferred_element_type=jnp.float32)
        * score_scale
    )
    d_query = rms_back(unrotate(d_qrot, tables), query_n, query_inv)
    d_key = rms_back(unrotate(d_krot, tables), key_n, key_inv)
    stacked = jnp.stack([d_query, d_key, d_values], 0)
    return (
        jnp.transpose(stacked, (2, 1, 0, 3))
        .reshape(length, groups * 3 * head_size)
        .astype(jnp.bfloat16)
    )


def on_device(latent, timesteps, positions, mod_weight, input_weight, output_weight, cotangent):
    width = latent.shape[2]
    groups = input_weight.shape[1]
    group_cols = groups * input_weight.shape[2]
    time_act = jax.nn.silu(time_embed(timesteps, width)).astype(jnp.bfloat16)
    slab_rows = mod_weight.shape[0]
    act_rows = lax.dynamic_slice_in_dim(time_act, lax.axis_index("cand") * slab_rows, slab_rows, 1)
    mod_mine = lax.psum_scatter(
        jnp.dot(act_rows, mod_weight, preferred_element_type=jnp.float32).astype(jnp.bfloat16),
        "cand",
        scatter_dimension=0,
        tiled=True,
    ).astype(jnp.float32)
    modulation = lax.all_gather(mod_mine, "seq", axis=1, tiled=True)[0]
    shift_vec = modulation[:width]
    scale_vec = modulation[width : 2 * width]
    gate_vec = modulation[2 * width :]
    latent_all = lax.all_gather(latent[0], "seq", axis=0, tiled=True)
    length = latent_all.shape[0]
    normed_all, _ = layer_norm(latent_all.astype(jnp.float32))
    modulated = (normed_all * (1.0 + scale_vec) + shift_vec).astype(jnp.bfloat16)
    tables = rope_tables(positions, HEAD)
    piece = lax.all_gather(input_weight, "cand", axis=0, tiled=True).reshape(width, group_cols)
    cot_all = lax.all_gather(cotangent[0], "seq", axis=0, tiled=True)
    w_heads = lax.all_gather(output_weight, "cand", axis=2, tiled=True)
    w_heads = w_heads.reshape(w_heads.shape[0] * w_heads.shape[1], width)
    projected = jnp.dot(modulated, piece, preferred_element_type=jnp.float32)
    attended, saved = attend(projected.reshape(length, groups, 3 * HEAD), tables)
    mixed_part = jnp.dot(attended, w_heads, preferred_element_type=jnp.float32).astype(jnp.bfloat16)
    mixed = lax.psum_scatter(mixed_part, "seq", scatter_dimension=0, tiled=True).astype(jnp.float32)
    latent_rows = latent[0].astype(jnp.float32)
    block_out = (latent_rows + gate_vec * mixed).astype(jnp.bfloat16)
    d_mixed = (cot_all.astype(jnp.float32) * gate_vec).astype(jnp.bfloat16)
    d_attended = times_transposed(d_mixed, w_heads).astype(jnp.bfloat16)
    d_projected = attend_back(d_attended, saved, tables)
    d_modulated = lax.psum_scatter(
        times_transposed(d_projected, piece).astype(jnp.bfloat16),
        "seq",
        scatter_dimension=0,
        tiled=True,
    ).astype(jnp.float32)
    normed, inverse_std = layer_norm(latent_rows)
    latent_grad = cotangent[0].astype(jnp.float32) + layer_norm_back(
        d_modulated * (1.0 + scale_vec), normed, inverse_std
    )
    return (block_out[None], latent_grad[None])


def solution(mesh):
    placed = (
        P("cand", "seq", None),
        P(),
        P(),
        P("cand", "seq"),
        P("cand", "seq", None),
        P("seq", None, "cand"),
        P("cand", "seq", None),
    )
    return jax.shard_map(
        on_device,
        mesh=mesh,
        in_specs=placed,
        out_specs=(P("cand", "seq", None), P("cand", "seq", None)),
        check_vma=False,
    )
```

```python
import functools

import jax
import jax.numpy as jnp
import numpy as np
from jax import lax
from jax.experimental import pallas as pl
from jax.experimental.pallas import tpu as pltpu
from jax.sharding import PartitionSpec as P

HEAD = 128
CHUNKS = 4
MESH = pl.DeviceIdType.MESH


epsilon = 1e-06


def time_embed(timesteps, feature_width):
    half_size = feature_width // 2
    freq_rate = jnp.exp(-jnp.log(10000.0) * jnp.arange(half_size, dtype=jnp.float32) / half_size)
    angles = timesteps.astype(jnp.float32)[:, None] * freq_rate[None, :]
    return jnp.concatenate([jnp.cos(angles), jnp.sin(angles)], axis=1)


def rope_tables(positions, head_size):
    first_size = head_size // 8
    other_size = (head_size - first_size) // 2
    pieces = []
    swapped = []
    sign_vec = []
    offset = 0
    for axis_id, width_part in enumerate((first_size, other_size, other_size)):
        half_size = width_part // 2
        freq_rate = jnp.exp(
            -jnp.log(256.0) * 2.0 * jnp.arange(half_size, dtype=jnp.float32) / width_part
        )
        angle_part = positions[axis_id].astype(jnp.float32)[:, None] * freq_rate[None, :]
        pieces.append(angle_part)
        pieces.append(angle_part)
        swapped += list(range(offset + half_size, offset + width_part)) + list(
            range(offset, offset + half_size)
        )
        sign_vec += [-1.0] * half_size + [1.0] * half_size
        offset += width_part
    angles = jnp.concatenate(pieces, axis=1)
    return (
        jnp.cos(angles),
        jnp.sin(angles),
        np.array(swapped, np.int32),
        np.array(sign_vec, np.float32),
    )


def swap_pairs(values):
    lane = lax.broadcasted_iota(jnp.int32, values.shape, 1)
    small = HEAD // 8
    large = (HEAD - small) // 2
    near = jnp.where(
        lane < small // 2,
        pltpu.roll(values, HEAD - small // 2, 1),
        pltpu.roll(values, small // 2, 1),
    )
    upper = ((lane >= small) & (lane < small + large // 2)) | (
        (lane >= small + large) & (lane < small + large + large // 2)
    )
    far = jnp.where(
        upper, pltpu.roll(values, HEAD - large // 2, 1), pltpu.roll(values, large // 2, 1)
    )
    return jnp.where(lane < small, near, far)


def dot_nt(left, right):
    return lax.dot_general(left, right, (((1,), (1,)), ((), ())), preferred_element_type=jnp.float32)


def dot_tn(left, right):
    return lax.dot_general(left, right, (((0,), (0,)), ((), ())), preferred_element_type=jnp.float32)


def inverse_rms(values):
    return lax.rsqrt(jnp.mean(values * values, -1, keepdims=True) + epsilon)


def layer_norm(values):
    centred = values - jnp.mean(values, -1, keepdims=True)
    inverse_std = lax.rsqrt(jnp.mean(centred * centred, -1, keepdims=True) + epsilon)
    return (centred * inverse_std, inverse_std)


def step_kernel(
    nc, ns,
    act_ref, cos_ref, sin_ref, mod_w_ref, latent_ref, cot_ref, w_in_ref, w_out_ref,
    block_ref, grad_ref,
    part, part_in, mine, mod_all, vecs,
    lat_all, cot_all, w_in_all, w_out_all, x_all, proj, q_all, k_all, v_all, probs, att, d_att,
    d_proj, mix_out, mix_in, dm_out, dm_in,
    own_sem, lat_s, lat_r, cot_s, cot_r, wi_s, wi_r, wo_s, wo_r, m1_s, m1_r, m2_s, m2_r,
    mx_s, mx_r, dm_s, dm_r,
):
    me_c = lax.axis_index("cand")
    me_s = lax.axis_index("seq")
    rows, width = latent_ref.shape
    length = rows * ns
    slab = w_in_ref.shape[0]
    groups = q_all.shape[0]
    cols = mod_w_ref.shape[1]
    piece = w_out_ref.shape[1]
    chunk = width // CHUNKS
    half = nc // 2
    mate = me_c + 1 - 2 * lax.rem(me_c, 2)
    score_scale = HEAD ** (-0.5)

    def seq_peer(k):
        return lax.rem(me_s + k, ns)

    def rows_of(index, size):
        return pl.ds(pl.multiple_of(index * size, size), size)

    def remote(src, dst, send, recv, cand, seq):
        copy = pltpu.make_async_remote_copy(
            src_ref=src, dst_ref=dst, send_sem=send, recv_sem=recv,
            device_id=(cand, seq), device_id_type=MESH,
        )
        copy.start()
        return copy

    barrier = pltpu.get_barrier_semaphore()
    for k in range(1, nc):
        pl.semaphore_signal(
            barrier, inc=1, device_id=(lax.rem(me_c + k, nc), me_s), device_id_type=MESH
        )
    for k in range(1, ns):
        pl.semaphore_signal(barrier, inc=1, device_id=(me_c, seq_peer(k)), device_id_type=MESH)

    own = [
        pltpu.make_async_copy(latent_ref, lat_all.at[rows_of(me_s, rows)], own_sem.at[0]),
        pltpu.make_async_copy(cot_ref, cot_all.at[rows_of(me_s, rows)], own_sem.at[1]),
        pltpu.make_async_copy(w_in_ref, w_in_all.at[rows_of(me_c, slab)], own_sem.at[2]),
        pltpu.make_async_copy(w_out_ref, w_out_all.at[me_c], own_sem.at[3]),
    ]
    for copy in own:
        copy.start()
    product = jnp.dot(act_ref[...], mod_w_ref[...], preferred_element_type=jnp.float32)
    for c in range(nc):
        part[c] = product[8 * c : 8 * c + 8]
    pl.semaphore_wait(barrier, nc - 1 + ns - 1)

    lat = [
        remote(latent_ref, lat_all.at[rows_of(me_s, rows)], lat_s.at[k], lat_r.at[k], me_c, seq_peer(k))
        for k in range(1, ns)
    ]
    m1 = []
    for k in range(1, nc):
        peer = lax.rem(me_c + k, nc)
        m1.append(remote(part.at[peer], part_in.at[me_c], m1_s.at[k], m1_r.at[k], peer, me_s))

    def cand_gather(src, place, send, recv):
        first = [remote(src, place(me_c), send.at[0], recv.at[0], mate, me_s)]
        for j in range(1, half):
            peer = lax.rem(me_c + 2 * j, nc)
            first.append(remote(src, place(me_c), send.at[j], recv.at[j], peer, me_s))
        return first

    def cand_forward(first, place, send, recv):
        second = []
        for j in range(1, half):
            first[j].wait_recv()
            held = place(lax.rem(me_c - 2 * j + nc, nc))
            second.append(remote(held, held, send.at[half + j], recv.at[half + j], mate, me_s))
        return second

    def in_place(index):
        return w_in_all.at[rows_of(index, slab)]

    def out_place(index):
        return w_out_all.at[index]

    w_in = cand_gather(w_in_ref, in_place, wi_s, wi_r)
    w_out = cand_gather(w_out_ref, out_place, wo_s, wo_r)

    for copy in m1:
        copy.wait_recv()
    total = part[me_c]
    for k in range(1, nc):
        total = total + part_in[lax.rem(me_c - k + nc, nc)]
    mine[...] = total
    mod_all[me_s] = total
    m2 = [
        remote(mine, mod_all.at[me_s], m2_s.at[k], m2_r.at[k], me_c, seq_peer(k))
        for k in range(1, ns)
    ]
    cot = [
        remote(cot_ref, cot_all.at[rows_of(me_s, rows)], cot_s.at[k], cot_r.at[k], me_c, seq_peer(k))
        for k in range(1, ns)
    ]
    for copy in lat + m2:
        copy.wait_recv()
    own[0].wait()
    for s in range(ns):
        at = s * cols
        while at < (s + 1) * cols:
            kind = at // width
            stop = min((s + 1) * cols, (kind + 1) * width)
            vecs[kind, :, at - kind * width : stop - kind * width] = mod_all[
                s, :, at - s * cols : stop - s * cols
            ]
            at = stop

    def norm_rows(index, _):
        at = rows_of(index, 16)
        normed, _inverse = layer_norm(lat_all[at].astype(jnp.float32))
        x_all[at] = (normed * (1.0 + vecs[1, 0:1]) + vecs[0, 0:1]).astype(jnp.bfloat16)
        return 0

    lax.fori_loop(0, length // 16, norm_rows, 0)
    w_in_second = cand_forward(w_in, in_place, wi_s, wi_r)
    w_in[0].wait_recv()
    own[2].wait()
    for copy in w_in_second:
        copy.wait_recv()
    w_out_second = cand_forward(w_out, out_place, wo_s, wo_r)

    tile = 3 * HEAD

    def project(index, _):
        at = pl.ds(pl.multiple_of(index * tile, tile), tile)
        proj[index] = jnp.dot(x_all[...], w_in_all[:, at], preferred_element_type=jnp.float32)
        return 0

    lax.fori_loop(0, groups, project, 0)

    def head_forward(h, _):
        query = proj[h, :, 0:HEAD]
        key = proj[h, :, HEAD : 2 * HEAD]
        query_n = query * inverse_rms(query)
        key_n = key * inverse_rms(key)
        q_rot = (query_n * cos_ref[...] + swap_pairs(query_n) * sin_ref[...]).astype(jnp.bfloat16)
        k_rot = (key_n * cos_ref[...] + swap_pairs(key_n) * sin_ref[...]).astype(jnp.bfloat16)
        values = proj[h, :, 2 * HEAD :].astype(jnp.bfloat16)
        q_all[h] = q_rot
        k_all[h] = k_rot
        v_all[h] = values
        weights = jnp.exp(dot_nt(q_rot, k_rot) * score_scale - HEAD**0.5)
        share = weights * (1.0 / jnp.sum(weights, -1, keepdims=True))
        probs[h] = share
        att[h] = jnp.dot(
            share.astype(jnp.bfloat16), values, preferred_element_type=jnp.float32
        ).astype(jnp.bfloat16)
        return 0

    lax.fori_loop(0, groups, head_forward, 0)

    own[3].wait()
    w_out[0].wait_recv()
    for copy in w_out_second:
        copy.wait_recv()

    def scatter(out, into, send, recv, j):
        copies = []
        for k in range(1, ns):
            peer = seq_peer(k)
            copies.append(
                remote(out.at[j, rows_of(peer, rows)], into.at[j, me_s], send.at[j, k], recv.at[j, k], me_c, peer)
            )
        return copies

    mixed = []
    per_chunk = chunk // piece
    for j in range(CHUNKS):
        for i in range(per_chunk):
            c = j * per_chunk + i
            block = jnp.zeros((length, piece), jnp.float32)
            for h in range(groups):
                block = block + jnp.dot(
                    att[h], w_out_all[c, h * HEAD : (h + 1) * HEAD], preferred_element_type=jnp.float32
                )
            mix_out[j, :, i * piece : (i + 1) * piece] = block.astype(jnp.bfloat16)
        mixed.append(scatter(mix_out, mix_in, mx_s, mx_r, j))

    for copy in cot:
        copy.wait_recv()
    own[1].wait()

    def gate_rows(index, _):
        at = rows_of(index, 16)
        x_all[at] = (cot_all[at].astype(jnp.float32) * vecs[2, 0:1]).astype(jnp.bfloat16)
        return 0

    lax.fori_loop(0, length // 16, gate_rows, 0)
    for h in range(groups):
        block = jnp.zeros((length, HEAD), jnp.float32)
        for c in range(nc):
            block = block + dot_nt(
                x_all[:, c * piece : (c + 1) * piece], w_out_all[c, h * HEAD : (h + 1) * HEAD]
            )
        d_att[h] = block.astype(jnp.bfloat16)

    def back_norm(d_rot, raw):
        inverse = inverse_rms(raw)
        normed = raw * inverse
        d_normed = d_rot * cos_ref[...] - swap_pairs(d_rot) * sin_ref[...]
        return inverse * (d_normed - normed * jnp.mean(d_normed * normed, -1, keepdims=True))

    def head_backward(h, _):
        d_heads = d_att[h]
        share = probs[h]
        d_values = dot_tn(share.astype(jnp.bfloat16), d_heads)
        d_probs = dot_nt(d_heads, v_all[h])
        d_scores = (share * (d_probs - jnp.sum(share * d_probs, -1, keepdims=True))).astype(
            jnp.bfloat16
        )
        d_qrot = jnp.dot(d_scores, k_all[h], preferred_element_type=jnp.float32) * score_scale
        d_krot = dot_tn(d_scores, q_all[h]) * score_scale
        d_query = back_norm(d_qrot, proj[h, :, 0:HEAD])
        d_key = back_norm(d_krot, proj[h, :, HEAD : 2 * HEAD])
        d_proj[h, :, 0:HEAD] = d_query.astype(jnp.bfloat16)
        d_proj[h, :, HEAD : 2 * HEAD] = d_key.astype(jnp.bfloat16)
        d_proj[h, :, 2 * HEAD :] = d_values.astype(jnp.bfloat16)
        return 0

    lax.fori_loop(0, groups, head_backward, 0)

    d_mod = []
    for j in range(CHUNKS):
        block = jnp.zeros((length, chunk), jnp.float32)
        for h in range(groups):
            block = block + dot_nt(
                d_proj[h], w_in_all[j * chunk : (j + 1) * chunk, h * tile : (h + 1) * tile]
            )
        dm_out[j] = block.astype(jnp.bfloat16)
        d_mod.append(scatter(dm_out, dm_in, dm_s, dm_r, j))

    def summed(out, into, j, at):
        start = pl.multiple_of(me_s * rows, rows) + at
        result = out[j, pl.ds(pl.multiple_of(start, 16), 16)].astype(jnp.float32)
        for k in range(1, ns):
            result = result + into[j, lax.rem(me_s + k, ns), at : at + 16].astype(jnp.float32)
        return result

    for j in range(CHUNKS):
        for copy in mixed[j]:
            copy.wait_recv()
    for at in range(0, rows, 16):
        for j in range(CHUNKS):
            part_cols = slice(j * chunk, (j + 1) * chunk)
            own_rows = pl.ds(pl.multiple_of(me_s * rows + at, 16), 16)
            block_ref[at : at + 16, part_cols] = (
                lat_all[own_rows, part_cols].astype(jnp.float32)
                + vecs[2, 0:1, part_cols] * summed(mix_out, mix_in, j, at)
            ).astype(jnp.bfloat16)

    for j in range(CHUNKS):
        for copy in d_mod[j]:
            copy.wait_recv()
    for at in range(0, rows, 16):
        own_rows = pl.ds(pl.multiple_of(me_s * rows + at, 16), 16)
        normed, inverse_std = layer_norm(lat_all[own_rows].astype(jnp.float32))
        d_normed = jnp.concatenate(
            [summed(dm_out, dm_in, j, at) for j in range(CHUNKS)], axis=1
        ) * (1.0 + vecs[1, 0:1])
        grad_ref[at : at + 16] = cot_all[own_rows].astype(jnp.float32) + inverse_std * (
            d_normed
            - jnp.mean(d_normed, -1, keepdims=True)
            - normed * jnp.mean(d_normed * normed, -1, keepdims=True)
        )

    for copy in lat + m1 + m2 + cot + w_in + w_out + w_in_second + w_out_second:
        copy.wait_send()
    for j in range(CHUNKS):
        for copy in mixed[j] + d_mod[j]:
            copy.wait_send()


def on_device(latent, timesteps, positions, mod_weight, input_weight, output_weight, cotangent):
    nc = lax.axis_size("cand")
    ns = lax.axis_size("seq")
    rows, width = latent.shape[1:]
    length = rows * ns
    slab = input_weight.shape[0]
    groups = input_weight.shape[1]
    cols = mod_weight.shape[1]
    piece = output_weight.shape[2]
    chunk = width // CHUNKS
    time_act = jax.nn.silu(time_embed(timesteps, width)).astype(jnp.bfloat16)
    act_rows = lax.dynamic_slice_in_dim(time_act, lax.axis_index("cand") * slab, slab, 1)
    act_rows = jnp.repeat(act_rows, 8, axis=0)
    cos_tab, sin_tab, _swapped, sign_vec = rope_tables(positions, HEAD)
    vmem = pl.BlockSpec(memory_space=pltpu.VMEM)
    anywhere = pl.BlockSpec(memory_space=pl.ANY)
    f32, bf16 = jnp.float32, jnp.bfloat16
    dma = pltpu.SemaphoreType.DMA
    block_out, latent_grad = pl.pallas_call(
        functools.partial(step_kernel, nc, ns),
        out_shape=(
            jax.ShapeDtypeStruct((rows, width), bf16),
            jax.ShapeDtypeStruct((rows, width), f32),
        ),
        in_specs=[vmem] * 4 + [anywhere] * 4,
        out_specs=(vmem, vmem),
        scratch_shapes=[
            pltpu.VMEM((nc, 8, cols), f32),
            pltpu.VMEM((nc, 8, cols), f32),
            pltpu.VMEM((8, cols), f32),
            pltpu.VMEM((ns, 8, cols), f32),
            pltpu.VMEM((3, 8, width), f32),
            pltpu.VMEM((length, width), bf16),
            pltpu.VMEM((length, width), bf16),
            pltpu.VMEM((slab * nc, groups * 3 * HEAD), bf16),
            pltpu.VMEM((nc, groups * HEAD, piece), bf16),
            pltpu.VMEM((length, width), bf16),
            pltpu.VMEM((groups, length, 3 * HEAD), f32),
            pltpu.VMEM((groups, length, HEAD), bf16),
            pltpu.VMEM((groups, length, HEAD), bf16),
            pltpu.VMEM((groups, length, HEAD), bf16),
            pltpu.VMEM((groups, length, length), f32),
            pltpu.VMEM((groups, length, HEAD), bf16),
            pltpu.VMEM((groups, length, HEAD), bf16),
            pltpu.VMEM((groups, length, 3 * HEAD), bf16),
            pltpu.VMEM((CHUNKS, length, chunk), bf16),
            pltpu.VMEM((CHUNKS, ns, rows, chunk), bf16),
            pltpu.VMEM((CHUNKS, length, chunk), bf16),
            pltpu.VMEM((CHUNKS, ns, rows, chunk), bf16),
            dma((4,)),
            dma((ns,)), dma((ns,)), dma((ns,)), dma((ns,)),
            dma((nc,)), dma((nc,)), dma((nc,)), dma((nc,)),
            dma((nc,)), dma((nc,)), dma((ns,)), dma((ns,)),
            dma((CHUNKS, ns)), dma((CHUNKS, ns)), dma((CHUNKS, ns)), dma((CHUNKS, ns)),
        ],
        compiler_params=pltpu.CompilerParams(
            collective_id=0, has_side_effects=True, vmem_limit_bytes=66000000
        ),
    )(
        act_rows, cos_tab, sin_tab * sign_vec, mod_weight, latent[0], cotangent[0],
        input_weight.reshape(slab, groups * 3 * HEAD),
        output_weight.reshape(groups * HEAD, piece),
    )
    return (block_out[None], latent_grad[None])


def solution(mesh):
    placed = (
        P("cand", "seq", None),
        P(),
        P(),
        P("cand", "seq"),
        P("cand", "seq", None),
        P("seq", None, "cand"),
        P("cand", "seq", None),
    )
    return jax.shard_map(
        on_device,
        mesh=mesh,
        in_specs=placed,
        out_specs=(P("cand", "seq", None), P("cand", "seq", None)),
        check_vma=False,
    )
```

```python
import functools

import jax
import jax.numpy as jnp
import numpy as np
from jax import lax
from jax.experimental import pallas as pl
from jax.experimental.pallas import tpu as pltpu
from jax.sharding import PartitionSpec as P

HEAD = 128
CHUNKS = 4
MESH = pl.DeviceIdType.MESH


epsilon = 1e-06


def time_embed(timesteps, feature_width):
    half_size = feature_width // 2
    freq_rate = jnp.exp(-jnp.log(10000.0) * jnp.arange(half_size, dtype=jnp.float32) / half_size)
    angles = timesteps.astype(jnp.float32)[:, None] * freq_rate[None, :]
    return jnp.concatenate([jnp.cos(angles), jnp.sin(angles)], axis=1)


def rope_tables(positions, head_size):
    first_size = head_size // 8
    other_size = (head_size - first_size) // 2
    pieces = []
    swapped = []
    sign_vec = []
    offset = 0
    for axis_id, width_part in enumerate((first_size, other_size, other_size)):
        half_size = width_part // 2
        freq_rate = jnp.exp(
            -jnp.log(256.0) * 2.0 * jnp.arange(half_size, dtype=jnp.float32) / width_part
        )
        angle_part = positions[axis_id].astype(jnp.float32)[:, None] * freq_rate[None, :]
        pieces.append(angle_part)
        pieces.append(angle_part)
        swapped += list(range(offset + half_size, offset + width_part)) + list(
            range(offset, offset + half_size)
        )
        sign_vec += [-1.0] * half_size + [1.0] * half_size
        offset += width_part
    angles = jnp.concatenate(pieces, axis=1)
    return (
        jnp.cos(angles),
        jnp.sin(angles),
        np.array(swapped, np.int32),
        np.array(sign_vec, np.float32),
    )


def swap_pairs(values):
    lane = lax.broadcasted_iota(jnp.int32, values.shape, 1)
    small = HEAD // 8
    large = (HEAD - small) // 2
    near = jnp.where(
        lane < small // 2,
        pltpu.roll(values, HEAD - small // 2, 1),
        pltpu.roll(values, small // 2, 1),
    )
    upper = ((lane >= small) & (lane < small + large // 2)) | (
        (lane >= small + large) & (lane < small + large + large // 2)
    )
    far = jnp.where(
        upper, pltpu.roll(values, HEAD - large // 2, 1), pltpu.roll(values, large // 2, 1)
    )
    return jnp.where(lane < small, near, far)


def dot_nt(left, right):
    return lax.dot_general(left, right, (((1,), (1,)), ((), ())), preferred_element_type=jnp.float32)


def dot_tn(left, right):
    return lax.dot_general(left, right, (((0,), (0,)), ((), ())), preferred_element_type=jnp.float32)


def inverse_rms(values):
    return lax.rsqrt(jnp.mean(values * values, -1, keepdims=True) + epsilon)


def layer_norm(values):
    centred = values - jnp.mean(values, -1, keepdims=True)
    inverse_std = lax.rsqrt(jnp.mean(centred * centred, -1, keepdims=True) + epsilon)
    return (centred * inverse_std, inverse_std)


def step_kernel(
    nc, ns,
    act_ref, cos_ref, sin_ref, mod_w_ref, latent_ref, cot_ref, w_in_ref, w_out_ref,
    block_ref, grad_ref,
    part, part_in, mine, mod_all, vecs,
    lat_all, cot_all, w_in_all, w_out_all, x_all, proj, q_all, k_all, v_all, probs, att, d_att,
    d_proj, mix_out, mix_near, mix_sum, mix_in, dm_out, dm_near, dm_sum, dm_in,
    own_sem, lat_s, lat_r, cot_s, cot_r, wi_s, wi_r, wo_s, wo_r, m1_s, m1_r, m2_s, m2_r,
    mxn_s, mxn_r, mx_s, mx_r, dmn_s, dmn_r, dm_s, dm_r,
):
    me_c = lax.axis_index("cand")
    me_s = lax.axis_index("seq")
    rows, width = latent_ref.shape
    length = rows * ns
    slab = w_in_ref.shape[0]
    groups = q_all.shape[0]
    cols = mod_w_ref.shape[1]
    piece = w_out_ref.shape[1]
    chunk = width // CHUNKS
    half = nc // 2
    mate = me_c + 1 - 2 * lax.rem(me_c, 2)
    far = ns // 2
    me_y, me_z = lax.rem(me_s, 2), lax.div(me_s, 2)
    near = me_s + 1 - 2 * me_y
    score_scale = HEAD ** (-0.5)

    def seq_peer(k):
        return lax.rem(me_s + k, ns)

    def place(index):
        return lax.rem(index, 2) * far + lax.div(index, 2)

    def rows_of(index, size):
        return pl.ds(pl.multiple_of(index * size, size), size)

    def remote(src, dst, send, recv, cand, seq):
        copy = pltpu.make_async_remote_copy(
            src_ref=src, dst_ref=dst, send_sem=send, recv_sem=recv,
            device_id=(cand, seq), device_id_type=MESH,
        )
        copy.start()
        return copy

    barrier = pltpu.get_barrier_semaphore()
    for k in range(1, nc):
        pl.semaphore_signal(
            barrier, inc=1, device_id=(lax.rem(me_c + k, nc), me_s), device_id_type=MESH
        )
    for k in range(1, ns):
        pl.semaphore_signal(barrier, inc=1, device_id=(me_c, seq_peer(k)), device_id_type=MESH)

    own = [
        pltpu.make_async_copy(latent_ref, lat_all.at[rows_of(place(me_s), rows)], own_sem.at[0]),
        pltpu.make_async_copy(cot_ref, cot_all.at[rows_of(place(me_s), rows)], own_sem.at[1]),
        pltpu.make_async_copy(w_in_ref, w_in_all.at[rows_of(me_c, slab)], own_sem.at[2]),
        pltpu.make_async_copy(w_out_ref, w_out_all.at[me_c], own_sem.at[3]),
    ]
    for copy in own:
        copy.start()
    product = jnp.dot(act_ref[...], mod_w_ref[...], preferred_element_type=jnp.float32)
    for c in range(nc):
        part[c] = product[8 * c : 8 * c + 8]
    pl.semaphore_wait(barrier, nc - 1 + ns - 1)

    def seq_gather(src, whole, send, recv):
        mine_there = whole.at[rows_of(place(me_s), rows)]
        first = [remote(src, mine_there, send.at[0], recv.at[0], me_c, near)]
        for j in range(1, far):
            first.append(remote(src, mine_there, send.at[j], recv.at[j], me_c, seq_peer(2 * j)))
        return first

    def seq_forward(first, whole, send, recv):
        second = []
        for j in range(1, far):
            first[j].wait_recv()
            held = whole.at[rows_of(place(seq_peer(ns - 2 * j)), rows)]
            second.append(remote(held, held, send.at[far + j], recv.at[far + j], me_c, near))
        return second

    lat = seq_gather(latent_ref, lat_all, lat_s, lat_r)
    m1 = []
    for k in range(1, nc):
        peer = lax.rem(me_c + k, nc)
        m1.append(remote(part.at[peer], part_in.at[me_c], m1_s.at[k], m1_r.at[k], peer, me_s))

    def cand_gather(src, spot, send, recv):
        first = [remote(src, spot(me_c), send.at[0], recv.at[0], mate, me_s)]
        for j in range(1, half):
            peer = lax.rem(me_c + 2 * j, nc)
            first.append(remote(src, spot(me_c), send.at[j], recv.at[j], peer, me_s))
        return first

    def cand_forward(first, spot, send, recv):
        second = []
        for j in range(1, half):
            first[j].wait_recv()
            held = spot(lax.rem(me_c - 2 * j + nc, nc))
            second.append(remote(held, held, send.at[half + j], recv.at[half + j], mate, me_s))
        return second

    def in_place(index):
        return w_in_all.at[rows_of(index, slab)]

    def out_place(index):
        return w_out_all.at[index]

    w_in = cand_gather(w_in_ref, in_place, wi_s, wi_r)
    w_out = cand_gather(w_out_ref, out_place, wo_s, wo_r)

    for copy in m1:
        copy.wait_recv()
    total = part[me_c]
    for k in range(1, nc):
        total = total + part_in[lax.rem(me_c - k + nc, nc)]
    mine[...] = total
    mod_all[me_s] = total
    m2 = [
        remote(mine, mod_all.at[me_s], m2_s.at[k], m2_r.at[k], me_c, seq_peer(k))
        for k in range(1, ns)
    ]
    lat_second = seq_forward(lat, lat_all, lat_s, lat_r)
    cot = seq_gather(cot_ref, cot_all, cot_s, cot_r)
    lat[0].wait_recv()
    for copy in lat_second + m2:
        copy.wait_recv()
    own[0].wait()
    for s in range(ns):
        at = s * cols
        while at < (s + 1) * cols:
            kind = at // width
            stop = min((s + 1) * cols, (kind + 1) * width)
            vecs[kind, :, at - kind * width : stop - kind * width] = mod_all[
                s, :, at - s * cols : stop - s * cols
            ]
            at = stop

    def norm_rows(index, _):
        at = rows_of(index, 16)
        normed, _inverse = layer_norm(lat_all[at].astype(jnp.float32))
        x_all[at] = (normed * (1.0 + vecs[1, 0:1]) + vecs[0, 0:1]).astype(jnp.bfloat16)
        return 0

    lax.fori_loop(0, length // 16, norm_rows, 0)
    w_in_second = cand_forward(w_in, in_place, wi_s, wi_r)
    w_in[0].wait_recv()
    own[2].wait()
    for copy in w_in_second:
        copy.wait_recv()
    w_out_second = cand_forward(w_out, out_place, wo_s, wo_r)

    tile = 3 * HEAD

    def project(index, _):
        at = pl.ds(pl.multiple_of(index * tile, tile), tile)
        proj[index] = jnp.dot(x_all[...], w_in_all[:, at], preferred_element_type=jnp.float32)
        return 0

    lax.fori_loop(0, groups, project, 0)

    def head_forward(h, _):
        query = proj[h, :, 0:HEAD]
        key = proj[h, :, HEAD : 2 * HEAD]
        query_n = query * inverse_rms(query)
        key_n = key * inverse_rms(key)
        q_rot = (query_n * cos_ref[...] + swap_pairs(query_n) * sin_ref[...]).astype(jnp.bfloat16)
        k_rot = (key_n * cos_ref[...] + swap_pairs(key_n) * sin_ref[...]).astype(jnp.bfloat16)
        values = proj[h, :, 2 * HEAD :].astype(jnp.bfloat16)
        q_all[h] = q_rot
        k_all[h] = k_rot
        v_all[h] = values
        weights = jnp.exp(dot_nt(q_rot, k_rot) * score_scale - HEAD**0.5)
        share = weights * (1.0 / jnp.sum(weights, -1, keepdims=True))
        probs[h] = share
        att[h] = jnp.dot(
            share.astype(jnp.bfloat16), values, preferred_element_type=jnp.float32
        ).astype(jnp.bfloat16)
        return 0

    lax.fori_loop(0, groups, head_forward, 0)

    own[3].wait()
    w_out[0].wait_recv()
    for copy in w_out_second:
        copy.wait_recv()

    def scatter_near(out, into, send, recv, j):
        away = out.at[j, rows_of(1 - me_y, far * rows)]
        return remote(away, into.at[j], send.at[j], recv.at[j], me_c, near)

    def scatter_far(first, out, into, sums, landed, send, recv, j):
        first.wait_recv()
        here = out[j, rows_of(me_y, far * rows)].astype(jnp.float32)
        sums[j] = (here + into[j].astype(jnp.float32)).astype(jnp.bfloat16)
        copies = []
        for k in range(1, far):
            peer = lax.rem(me_z + k, far)
            copies.append(
                remote(
                    sums.at[j, rows_of(peer, rows)], landed.at[j, me_z],
                    send.at[j, k], recv.at[j, k], me_c, 2 * peer + me_y,
                )
            )
        return copies

    cot_second = seq_forward(cot, cot_all, cot_s, cot_r)
    mixed_near = []
    per_chunk = chunk // piece
    for j in range(CHUNKS):
        for i in range(per_chunk):
            c = j * per_chunk + i
            block = jnp.zeros((length, piece), jnp.float32)
            for h in range(groups):
                block = block + jnp.dot(
                    att[h], w_out_all[c, h * HEAD : (h + 1) * HEAD], preferred_element_type=jnp.float32
                )
            mix_out[j, :, i * piece : (i + 1) * piece] = block.astype(jnp.bfloat16)
        mixed_near.append(scatter_near(mix_out, mix_near, mxn_s, mxn_r, j))

    cot[0].wait_recv()
    for copy in cot_second:
        copy.wait_recv()
    own[1].wait()

    def gate_rows(index, _):
        at = rows_of(index, 16)
        x_all[at] = (cot_all[at].astype(jnp.float32) * vecs[2, 0:1]).astype(jnp.bfloat16)
        return 0

    lax.fori_loop(0, length // 16, gate_rows, 0)
    for h in range(groups):
        block = jnp.zeros((length, HEAD), jnp.float32)
        for c in range(nc):
            block = block + dot_nt(
                x_all[:, c * piece : (c + 1) * piece], w_out_all[c, h * HEAD : (h + 1) * HEAD]
            )
        d_att[h] = block.astype(jnp.bfloat16)

    def back_norm(d_rot, raw):
        inverse = inverse_rms(raw)
        normed = raw * inverse
        d_normed = d_rot * cos_ref[...] - swap_pairs(d_rot) * sin_ref[...]
        return inverse * (d_normed - normed * jnp.mean(d_normed * normed, -1, keepdims=True))

    def head_backward(h, _):
        d_heads = d_att[h]
        share = probs[h]
        d_values = dot_tn(share.astype(jnp.bfloat16), d_heads)
        d_probs = dot_nt(d_heads, v_all[h])
        d_scores = (share * (d_probs - jnp.sum(share * d_probs, -1, keepdims=True))).astype(
            jnp.bfloat16
        )
        d_qrot = jnp.dot(d_scores, k_all[h], preferred_element_type=jnp.float32) * score_scale
        d_krot = dot_tn(d_scores, q_all[h]) * score_scale
        d_query = back_norm(d_qrot, proj[h, :, 0:HEAD])
        d_key = back_norm(d_krot, proj[h, :, HEAD : 2 * HEAD])
        d_proj[h, :, 0:HEAD] = d_query.astype(jnp.bfloat16)
        d_proj[h, :, HEAD : 2 * HEAD] = d_key.astype(jnp.bfloat16)
        d_proj[h, :, 2 * HEAD :] = d_values.astype(jnp.bfloat16)
        return 0

    lax.fori_loop(0, groups, head_backward, 0)

    d_near = []
    mixed = []
    for j in range(CHUNKS):
        block = jnp.zeros((length, chunk), jnp.float32)
        for h in range(groups):
            block = block + dot_nt(
                d_proj[h], w_in_all[j * chunk : (j + 1) * chunk, h * tile : (h + 1) * tile]
            )
        dm_out[j] = block.astype(jnp.bfloat16)
        d_near.append(scatter_near(dm_out, dm_near, dmn_s, dmn_r, j))
        mixed.append(
            scatter_far(mixed_near[j], mix_out, mix_near, mix_sum, mix_in, mx_s, mx_r, j)
        )
    d_mod = [
        scatter_far(d_near[j], dm_out, dm_near, dm_sum, dm_in, dm_s, dm_r, j)
        for j in range(CHUNKS)
    ]

    def summed(sums, landed, j, at):
        start = pl.multiple_of(me_z * rows, rows) + at
        result = sums[j, pl.ds(pl.multiple_of(start, 16), 16)].astype(jnp.float32)
        for k in range(1, far):
            result = result + landed[j, lax.rem(me_z + k, far), at : at + 16].astype(jnp.float32)
        return result

    for j in range(CHUNKS):
        for copy in mixed[j]:
            copy.wait_recv()
    for at in range(0, rows, 16):
        for j in range(CHUNKS):
            part_cols = slice(j * chunk, (j + 1) * chunk)
            own_rows = pl.ds(pl.multiple_of(place(me_s) * rows + at, 16), 16)
            block_ref[at : at + 16, part_cols] = (
                lat_all[own_rows, part_cols].astype(jnp.float32)
                + vecs[2, 0:1, part_cols] * summed(mix_sum, mix_in, j, at)
            ).astype(jnp.bfloat16)

    for j in range(CHUNKS):
        for copy in d_mod[j]:
            copy.wait_recv()
    for at in range(0, rows, 16):
        own_rows = pl.ds(pl.multiple_of(place(me_s) * rows + at, 16), 16)
        normed, inverse_std = layer_norm(lat_all[own_rows].astype(jnp.float32))
        d_normed = jnp.concatenate(
            [summed(dm_sum, dm_in, j, at) for j in range(CHUNKS)], axis=1
        ) * (1.0 + vecs[1, 0:1])
        grad_ref[at : at + 16] = cot_all[own_rows].astype(jnp.float32) + inverse_std * (
            d_normed
            - jnp.mean(d_normed, -1, keepdims=True)
            - normed * jnp.mean(d_normed * normed, -1, keepdims=True)
        )

    for copy in (
        lat + lat_second + m1 + m2 + cot + cot_second + w_in + w_out + w_in_second + w_out_second
        + mixed_near + d_near
    ):
        copy.wait_send()
    for j in range(CHUNKS):
        for copy in mixed[j] + d_mod[j]:
            copy.wait_send()


def on_device(latent, timesteps, positions, mod_weight, input_weight, output_weight, cotangent):
    nc = lax.axis_size("cand")
    ns = lax.axis_size("seq")
    rows, width = latent.shape[1:]
    length = rows * ns
    slab = input_weight.shape[0]
    groups = input_weight.shape[1]
    cols = mod_weight.shape[1]
    piece = output_weight.shape[2]
    chunk = width // CHUNKS
    time_act = jax.nn.silu(time_embed(timesteps, width)).astype(jnp.bfloat16)
    act_rows = lax.dynamic_slice_in_dim(time_act, lax.axis_index("cand") * slab, slab, 1)
    act_rows = jnp.repeat(act_rows, 8, axis=0)
    ordered = positions.reshape(-1, ns // 2, 2, rows).swapaxes(1, 2).reshape(-1, length)
    cos_tab, sin_tab, _swapped, sign_vec = rope_tables(ordered, HEAD)
    vmem = pl.BlockSpec(memory_space=pltpu.VMEM)
    anywhere = pl.BlockSpec(memory_space=pl.ANY)
    f32, bf16 = jnp.float32, jnp.bfloat16
    dma = pltpu.SemaphoreType.DMA
    block_out, latent_grad = pl.pallas_call(
        functools.partial(step_kernel, nc, ns),
        out_shape=(
            jax.ShapeDtypeStruct((rows, width), bf16),
            jax.ShapeDtypeStruct((rows, width), f32),
        ),
        in_specs=[vmem] * 4 + [anywhere] * 4,
        out_specs=(vmem, vmem),
        scratch_shapes=[
            pltpu.VMEM((nc, 8, cols), f32),
            pltpu.VMEM((nc, 8, cols), f32),
            pltpu.VMEM((8, cols), f32),
            pltpu.VMEM((ns, 8, cols), f32),
            pltpu.VMEM((3, 8, width), f32),
            pltpu.VMEM((length, width), bf16),
            pltpu.VMEM((length, width), bf16),
            pltpu.VMEM((slab * nc, groups * 3 * HEAD), bf16),
            pltpu.VMEM((nc, groups * HEAD, piece), bf16),
            pltpu.VMEM((length, width), bf16),
            pltpu.VMEM((groups, length, 3 * HEAD), f32),
            pltpu.VMEM((groups, length, HEAD), bf16),
            pltpu.VMEM((groups, length, HEAD), bf16),
            pltpu.VMEM((groups, length, HEAD), bf16),
            pltpu.VMEM((groups, length, length), f32),
            pltpu.VMEM((groups, length, HEAD), bf16),
            pltpu.VMEM((groups, length, HEAD), bf16),
            pltpu.VMEM((groups, length, 3 * HEAD), bf16),
            pltpu.VMEM((CHUNKS, length, chunk), bf16),
            pltpu.VMEM((CHUNKS, length // 2, chunk), bf16),
            pltpu.VMEM((CHUNKS, length // 2, chunk), bf16),
            pltpu.VMEM((CHUNKS, ns // 2, rows, chunk), bf16),
            pltpu.VMEM((CHUNKS, length, chunk), bf16),
            pltpu.VMEM((CHUNKS, length // 2, chunk), bf16),
            pltpu.VMEM((CHUNKS, length // 2, chunk), bf16),
            pltpu.VMEM((CHUNKS, ns // 2, rows, chunk), bf16),
            dma((4,)),
            dma((ns,)), dma((ns,)), dma((ns,)), dma((ns,)),
            dma((nc,)), dma((nc,)), dma((nc,)), dma((nc,)),
            dma((nc,)), dma((nc,)), dma((ns,)), dma((ns,)),
            dma((CHUNKS,)), dma((CHUNKS,)), dma((CHUNKS, ns // 2)), dma((CHUNKS, ns // 2)),
            dma((CHUNKS,)), dma((CHUNKS,)), dma((CHUNKS, ns // 2)), dma((CHUNKS, ns // 2)),
        ],
        compiler_params=pltpu.CompilerParams(
            collective_id=0, has_side_effects=True, vmem_limit_bytes=66000000
        ),
    )(
        act_rows, cos_tab, sin_tab * sign_vec, mod_weight, latent[0], cotangent[0],
        input_weight.reshape(slab, groups * 3 * HEAD),
        output_weight.reshape(groups * HEAD, piece),
    )
    return (block_out[None], latent_grad[None])


def solution(mesh):
    placed = (
        P("cand", "seq", None),
        P(),
        P(),
        P("cand", "seq"),
        P("cand", "seq", None),
        P("seq", None, "cand"),
        P("cand", "seq", None),
    )
    return jax.shard_map(
        on_device,
        mesh=mesh,
        in_specs=placed,
        out_specs=(P("cand", "seq", None), P("cand", "seq", None)),
        check_vma=False,
    )
```

```python
import functools

import jax
import jax.numpy as jnp
import numpy as np
from jax import lax
from jax.experimental import pallas as pl
from jax.experimental.pallas import tpu as pltpu
from jax.sharding import PartitionSpec as P

HEAD = 128
CHUNKS = 8
PIECE = 16
MESH = pl.DeviceIdType.MESH


epsilon = 1e-06


def time_embed(timesteps, feature_width):
    half_size = feature_width // 2
    freq_rate = jnp.exp(-jnp.log(10000.0) * jnp.arange(half_size, dtype=jnp.float32) / half_size)
    angles = timesteps.astype(jnp.float32)[:, None] * freq_rate[None, :]
    return jnp.concatenate([jnp.cos(angles), jnp.sin(angles)], axis=1)


def rope_tables(positions, head_size):
    first_size = head_size // 8
    other_size = (head_size - first_size) // 2
    pieces = []
    swapped = []
    sign_vec = []
    offset = 0
    for axis_id, width_part in enumerate((first_size, other_size, other_size)):
        half_size = width_part // 2
        freq_rate = jnp.exp(
            -jnp.log(256.0) * 2.0 * jnp.arange(half_size, dtype=jnp.float32) / width_part
        )
        angle_part = positions[axis_id].astype(jnp.float32)[:, None] * freq_rate[None, :]
        pieces.append(angle_part)
        pieces.append(angle_part)
        swapped += list(range(offset + half_size, offset + width_part)) + list(
            range(offset, offset + half_size)
        )
        sign_vec += [-1.0] * half_size + [1.0] * half_size
        offset += width_part
    angles = jnp.concatenate(pieces, axis=1)
    return (
        jnp.cos(angles),
        jnp.sin(angles),
        np.array(swapped, np.int32),
        np.array(sign_vec, np.float32),
    )


def swap_pairs(values):
    lane = lax.broadcasted_iota(jnp.int32, values.shape, 1)
    small = HEAD // 8
    large = (HEAD - small) // 2
    near = jnp.where(
        lane < small // 2,
        pltpu.roll(values, HEAD - small // 2, 1),
        pltpu.roll(values, small // 2, 1),
    )
    upper = ((lane >= small) & (lane < small + large // 2)) | (
        (lane >= small + large) & (lane < small + large + large // 2)
    )
    far = jnp.where(
        upper, pltpu.roll(values, HEAD - large // 2, 1), pltpu.roll(values, large // 2, 1)
    )
    return jnp.where(lane < small, near, far)


def dot_nt(left, right):
    return lax.dot_general(left, right, (((1,), (1,)), ((), ())), preferred_element_type=jnp.float32)


def dot_tn(left, right):
    return lax.dot_general(left, right, (((0,), (0,)), ((), ())), preferred_element_type=jnp.float32)


def inverse_rms(values):
    return lax.rsqrt(jnp.mean(values * values, -1, keepdims=True) + epsilon)


def layer_norm(values):
    centred = values - jnp.mean(values, -1, keepdims=True)
    inverse_std = lax.rsqrt(jnp.mean(centred * centred, -1, keepdims=True) + epsilon)
    return (centred * inverse_std, inverse_std)


def step_kernel(
    nc, ns,
    act_ref, cos_ref, sin_ref, mod_w_ref, latent_ref, cot_ref, w_in_ref, w_out_ref,
    block_ref, grad_ref,
    part, part_in, mine, mod_all, vecs,
    lat_all, cot_all, w_in_all, w_out_all, x_all, proj, q_all, k_all, v_all, probs, att, d_att,
    d_proj, mix_out, mix_near, mix_sum, mix_in, dm_out, dm_near, dm_sum, dm_in,
    own_sem, lat_s, lat_r, cot_s, cot_r, wi_s, wi_r, wo_s, wo_r, m1_s, m1_r, m2_s, m2_r,
    mxn_s, mxn_r, mx_s, mx_r, dmn_s, dmn_r, dm_s, dm_r,
):
    me_c = lax.axis_index("cand")
    me_s = lax.axis_index("seq")
    rows, width = latent_ref.shape
    length = rows * ns
    slab = w_in_ref.shape[0]
    groups = q_all.shape[0]
    cols = mod_w_ref.shape[1]
    piece = w_out_ref.shape[1]
    chunk = width // CHUNKS
    half = nc // 2
    mate = me_c + 1 - 2 * lax.rem(me_c, 2)
    far = ns // 2
    me_y, me_z = lax.rem(me_s, 2), lax.div(me_s, 2)
    near = me_s + 1 - 2 * me_y
    score_scale = HEAD ** (-0.5)

    def seq_peer(k):
        return lax.rem(me_s + k, ns)

    def place(index):
        return lax.rem(index, 2) * far + lax.div(index, 2)

    def rows_of(index, size):
        return pl.ds(pl.multiple_of(index * size, size), size)

    def remote(src, dst, send, recv, cand, seq):
        copy = pltpu.make_async_remote_copy(
            src_ref=src, dst_ref=dst, send_sem=send, recv_sem=recv,
            device_id=(cand, seq), device_id_type=MESH,
        )
        copy.start()
        return copy

    barrier = pltpu.get_barrier_semaphore()
    for k in range(1, nc):
        pl.semaphore_signal(
            barrier, inc=1, device_id=(lax.rem(me_c + k, nc), me_s), device_id_type=MESH
        )
    for k in range(1, ns):
        pl.semaphore_signal(barrier, inc=1, device_id=(me_c, seq_peer(k)), device_id_type=MESH)

    own = [
        pltpu.make_async_copy(latent_ref, lat_all.at[rows_of(place(me_s), rows)], own_sem.at[0]),
        pltpu.make_async_copy(cot_ref, cot_all.at[rows_of(place(me_s), rows)], own_sem.at[1]),
        pltpu.make_async_copy(w_in_ref, w_in_all.at[rows_of(me_c, slab)], own_sem.at[2]),
        pltpu.make_async_copy(w_out_ref, w_out_all.at[me_c], own_sem.at[3]),
    ]
    for copy in own:
        copy.start()
    product = jnp.dot(act_ref[...], mod_w_ref[...], preferred_element_type=jnp.float32)
    for c in range(nc):
        part[c] = product[8 * c : 8 * c + 8]
    pl.semaphore_wait(barrier, nc - 1 + ns - 1)

    pieces = rows // PIECE

    def piece_of(whole, index, p):
        return whole.at[pl.ds(pl.multiple_of(place(index) * rows + p * PIECE, PIECE), PIECE)]

    def seq_gather(src, whole, send, recv):
        near_copies, far_copies = [], []
        for p in range(pieces):
            from_here = src.at[pl.ds(p * PIECE, PIECE)]
            there = piece_of(whole, me_s, p)
            near_copies.append(
                remote(from_here, there, send.at[p, 0], recv.at[p, 0], me_c, near)
            )
            far_copies.append(
                [
                    remote(from_here, there, send.at[p, j], recv.at[p, j], me_c, seq_peer(2 * j))
                    for j in range(1, far)
                ]
            )
        return near_copies, far_copies

    def seq_forward(far_copies, whole, send, recv, p):
        second = []
        for j in range(1, far):
            far_copies[p][j - 1].wait_recv()
            held = piece_of(whole, seq_peer(ns - 2 * j), p)
            second.append(
                remote(held, held, send.at[p, far + j], recv.at[p, far + j], me_c, near)
            )
        return second

    lat_near, lat_far = seq_gather(latent_ref, lat_all, lat_s, lat_r)
    m1 = []
    for k in range(1, nc):
        peer = lax.rem(me_c + k, nc)
        m1.append(remote(part.at[peer], part_in.at[me_c], m1_s.at[k], m1_r.at[k], peer, me_s))

    def cand_gather(src, spot, send, recv):
        first = [remote(src, spot(me_c), send.at[0], recv.at[0], mate, me_s)]
        for j in range(1, half):
            peer = lax.rem(me_c + 2 * j, nc)
            first.append(remote(src, spot(me_c), send.at[j], recv.at[j], peer, me_s))
        return first

    def cand_forward(first, spot, send, recv):
        second = []
        for j in range(1, half):
            first[j].wait_recv()
            held = spot(lax.rem(me_c - 2 * j + nc, nc))
            second.append(remote(held, held, send.at[half + j], recv.at[half + j], mate, me_s))
        return second

    def in_place(index):
        return w_in_all.at[rows_of(index, slab)]

    def out_place(index):
        return w_out_all.at[index]

    w_in = cand_gather(w_in_ref, in_place, wi_s, wi_r)
    w_out = cand_gather(w_out_ref, out_place, wo_s, wo_r)

    for copy in m1:
        copy.wait_recv()
    total = part[me_c]
    for k in range(1, nc):
        total = total + part_in[lax.rem(me_c - k + nc, nc)]
    mine[...] = total
    mod_all[me_s] = total
    m2 = [
        remote(mine, mod_all.at[me_s], m2_s.at[k], m2_r.at[k], me_c, seq_peer(k))
        for k in range(1, ns)
    ]
    lat_second = []
    for p in range(pieces):
        lat_second += seq_forward(lat_far, lat_all, lat_s, lat_r, p)
    cot_near, cot_far = seq_gather(cot_ref, cot_all, cot_s, cot_r)
    cot_second = []
    for copy in lat_near + lat_second + m2:
        copy.wait_recv()
    own[0].wait()
    for s in range(ns):
        at = s * cols
        while at < (s + 1) * cols:
            kind = at // width
            stop = min((s + 1) * cols, (kind + 1) * width)
            vecs[kind, :, at - kind * width : stop - kind * width] = mod_all[
                s, :, at - s * cols : stop - s * cols
            ]
            at = stop

    def norm_rows(index, _):
        at = rows_of(index, 16)
        normed, _inverse = layer_norm(lat_all[at].astype(jnp.float32))
        x_all[at] = (normed * (1.0 + vecs[1, 0:1]) + vecs[0, 0:1]).astype(jnp.bfloat16)
        return 0

    lax.fori_loop(0, length // 16, norm_rows, 0)
    cot_second += seq_forward(cot_far, cot_all, cot_s, cot_r, 0)
    w_in_second = cand_forward(w_in, in_place, wi_s, wi_r)
    w_in[0].wait_recv()
    own[2].wait()
    for copy in w_in_second:
        copy.wait_recv()
    w_out_second = cand_forward(w_out, out_place, wo_s, wo_r)

    tile = 3 * HEAD

    def project(index, _):
        at = pl.ds(pl.multiple_of(index * tile, tile), tile)
        proj[index] = jnp.dot(x_all[...], w_in_all[:, at], preferred_element_type=jnp.float32)
        return 0

    lax.fori_loop(0, groups, project, 0)

    def head_forward(h, _):
        query = proj[h, :, 0:HEAD]
        key = proj[h, :, HEAD : 2 * HEAD]
        query_n = query * inverse_rms(query)
        key_n = key * inverse_rms(key)
        q_rot = (query_n * cos_ref[...] + swap_pairs(query_n) * sin_ref[...]).astype(jnp.bfloat16)
        k_rot = (key_n * cos_ref[...] + swap_pairs(key_n) * sin_ref[...]).astype(jnp.bfloat16)
        values = proj[h, :, 2 * HEAD :].astype(jnp.bfloat16)
        q_all[h] = q_rot
        k_all[h] = k_rot
        v_all[h] = values
        weights = jnp.exp(dot_nt(q_rot, k_rot) * score_scale - HEAD**0.5)
        share = weights * (1.0 / jnp.sum(weights, -1, keepdims=True))
        probs[h] = share
        att[h] = jnp.dot(
            share.astype(jnp.bfloat16), values, preferred_element_type=jnp.float32
        ).astype(jnp.bfloat16)
        return 0

    lax.fori_loop(0, groups, head_forward, 0)
    for p in range(1, pieces - 1):
        cot_second += seq_forward(cot_far, cot_all, cot_s, cot_r, p)

    own[3].wait()
    w_out[0].wait_recv()
    for copy in w_out_second:
        copy.wait_recv()

    def scatter_near(out, into, send, recv, j):
        away = out.at[j, rows_of(1 - me_y, far * rows)]
        return remote(away, into.at[j], send.at[j], recv.at[j], me_c, near)

    def scatter_far(first, out, into, sums, landed, send, recv, j):
        first.wait_recv()
        here = out[j, rows_of(me_y, far * rows)].astype(jnp.float32)
        sums[j] = (here + into[j].astype(jnp.float32)).astype(jnp.bfloat16)
        copies = []
        for k in range(1, far):
            peer = lax.rem(me_z + k, far)
            copies.append(
                remote(
                    sums.at[j, rows_of(peer, rows)], landed.at[j, me_z],
                    send.at[j, k], recv.at[j, k], me_c, 2 * peer + me_y,
                )
            )
        return copies

    mixed_near = []
    span = max(chunk, piece)
    for n in range(width // span):
        for i in range(span // piece):
            c = n * (span // piece) + i
            block = jnp.zeros((length, piece), jnp.float32)
            for h in range(groups):
                block = block + jnp.dot(
                    att[h], w_out_all[c, h * HEAD : (h + 1) * HEAD], preferred_element_type=jnp.float32
                )
            block = block.astype(jnp.bfloat16)
            if piece < chunk:
                mix_out[n, :, i * piece : (i + 1) * piece] = block
            else:
                for m in range(span // chunk):
                    mix_out[n * (span // chunk) + m] = block[:, m * chunk : (m + 1) * chunk]
        for m in range(span // chunk):
            j = n * (span // chunk) + m
            mixed_near.append(scatter_near(mix_out, mix_near, mxn_s, mxn_r, j))
        if n == 1:
            cot_second += seq_forward(cot_far, cot_all, cot_s, cot_r, pieces - 1)

    for copy in cot_near + cot_second:
        copy.wait_recv()
    own[1].wait()

    def gate_rows(index, _):
        at = rows_of(index, 16)
        x_all[at] = (cot_all[at].astype(jnp.float32) * vecs[2, 0:1]).astype(jnp.bfloat16)
        return 0

    lax.fori_loop(0, length // 16, gate_rows, 0)
    for h in range(groups):
        block = jnp.zeros((length, HEAD), jnp.float32)
        for c in range(nc):
            block = block + dot_nt(
                x_all[:, c * piece : (c + 1) * piece], w_out_all[c, h * HEAD : (h + 1) * HEAD]
            )
        d_att[h] = block.astype(jnp.bfloat16)

    def back_norm(d_rot, raw):
        inverse = inverse_rms(raw)
        normed = raw * inverse
        d_normed = d_rot * cos_ref[...] - swap_pairs(d_rot) * sin_ref[...]
        return inverse * (d_normed - normed * jnp.mean(d_normed * normed, -1, keepdims=True))

    def head_backward(h, _):
        d_heads = d_att[h]
        share = probs[h]
        d_values = dot_tn(share.astype(jnp.bfloat16), d_heads)
        d_probs = dot_nt(d_heads, v_all[h])
        d_scores = (share * (d_probs - jnp.sum(share * d_probs, -1, keepdims=True))).astype(
            jnp.bfloat16
        )
        d_qrot = jnp.dot(d_scores, k_all[h], preferred_element_type=jnp.float32) * score_scale
        d_krot = dot_tn(d_scores, q_all[h]) * score_scale
        d_query = back_norm(d_qrot, proj[h, :, 0:HEAD])
        d_key = back_norm(d_krot, proj[h, :, HEAD : 2 * HEAD])
        d_proj[h, :, 0:HEAD] = d_query.astype(jnp.bfloat16)
        d_proj[h, :, HEAD : 2 * HEAD] = d_key.astype(jnp.bfloat16)
        d_proj[h, :, 2 * HEAD :] = d_values.astype(jnp.bfloat16)
        return 0

    lax.fori_loop(0, groups, head_backward, 0)

    d_near = []
    mixed = []
    for j in range(CHUNKS):
        block = jnp.zeros((length, chunk), jnp.float32)
        for h in range(groups):
            block = block + dot_nt(
                d_proj[h], w_in_all[j * chunk : (j + 1) * chunk, h * tile : (h + 1) * tile]
            )
        dm_out[j] = block.astype(jnp.bfloat16)
        d_near.append(scatter_near(dm_out, dm_near, dmn_s, dmn_r, j))
        mixed.append(
            scatter_far(mixed_near[j], mix_out, mix_near, mix_sum, mix_in, mx_s, mx_r, j)
        )
    d_mod = [
        scatter_far(d_near[j], dm_out, dm_near, dm_sum, dm_in, dm_s, dm_r, j)
        for j in range(CHUNKS)
    ]

    def summed(sums, landed, j, at):
        start = pl.multiple_of(me_z * rows, rows) + at
        result = sums[j, pl.ds(pl.multiple_of(start, 16), 16)].astype(jnp.float32)
        for k in range(1, far):
            result = result + landed[j, lax.rem(me_z + k, far), at : at + 16].astype(jnp.float32)
        return result

    for j in range(CHUNKS):
        for copy in mixed[j]:
            copy.wait_recv()
    for at in range(0, rows, 16):
        for j in range(CHUNKS):
            part_cols = slice(j * chunk, (j + 1) * chunk)
            own_rows = pl.ds(pl.multiple_of(place(me_s) * rows + at, 16), 16)
            block_ref[at : at + 16, part_cols] = (
                lat_all[own_rows, part_cols].astype(jnp.float32)
                + vecs[2, 0:1, part_cols] * summed(mix_sum, mix_in, j, at)
            ).astype(jnp.bfloat16)

    for j in range(CHUNKS):
        for copy in d_mod[j]:
            copy.wait_recv()
    for at in range(0, rows, 16):
        own_rows = pl.ds(pl.multiple_of(place(me_s) * rows + at, 16), 16)
        normed, inverse_std = layer_norm(lat_all[own_rows].astype(jnp.float32))
        d_normed = jnp.concatenate(
            [summed(dm_sum, dm_in, j, at) for j in range(CHUNKS)], axis=1
        ) * (1.0 + vecs[1, 0:1])
        grad_ref[at : at + 16] = cot_all[own_rows].astype(jnp.float32) + inverse_std * (
            d_normed
            - jnp.mean(d_normed, -1, keepdims=True)
            - normed * jnp.mean(d_normed * normed, -1, keepdims=True)
        )

    for copy in (
        lat_near + lat_second + sum(lat_far, []) + m1 + m2 + cot_near + cot_second
        + sum(cot_far, []) + w_in + w_out + w_in_second + w_out_second
        + mixed_near + d_near
    ):
        copy.wait_send()
    for j in range(CHUNKS):
        for copy in mixed[j] + d_mod[j]:
            copy.wait_send()


def on_device(latent, timesteps, positions, mod_weight, input_weight, output_weight, cotangent):
    nc = lax.axis_size("cand")
    ns = lax.axis_size("seq")
    rows, width = latent.shape[1:]
    length = rows * ns
    slab = input_weight.shape[0]
    groups = input_weight.shape[1]
    cols = mod_weight.shape[1]
    piece = output_weight.shape[2]
    chunk = width // CHUNKS
    time_act = jax.nn.silu(time_embed(timesteps, width)).astype(jnp.bfloat16)
    act_rows = lax.dynamic_slice_in_dim(time_act, lax.axis_index("cand") * slab, slab, 1)
    act_rows = jnp.repeat(act_rows, 8, axis=0)
    ordered = positions.reshape(-1, ns // 2, 2, rows).swapaxes(1, 2).reshape(-1, length)
    cos_tab, sin_tab, _swapped, sign_vec = rope_tables(ordered, HEAD)
    vmem = pl.BlockSpec(memory_space=pltpu.VMEM)
    anywhere = pl.BlockSpec(memory_space=pl.ANY)
    f32, bf16 = jnp.float32, jnp.bfloat16
    dma = pltpu.SemaphoreType.DMA
    block_out, latent_grad = pl.pallas_call(
        functools.partial(step_kernel, nc, ns),
        out_shape=(
            jax.ShapeDtypeStruct((rows, width), bf16),
            jax.ShapeDtypeStruct((rows, width), f32),
        ),
        in_specs=[vmem] * 4 + [anywhere] * 4,
        out_specs=(vmem, vmem),
        scratch_shapes=[
            pltpu.VMEM((nc, 8, cols), f32),
            pltpu.VMEM((nc, 8, cols), f32),
            pltpu.VMEM((8, cols), f32),
            pltpu.VMEM((ns, 8, cols), f32),
            pltpu.VMEM((3, 8, width), f32),
            pltpu.VMEM((length, width), bf16),
            pltpu.VMEM((length, width), bf16),
            pltpu.VMEM((slab * nc, groups * 3 * HEAD), bf16),
            pltpu.VMEM((nc, groups * HEAD, piece), bf16),
            pltpu.VMEM((length, width), bf16),
            pltpu.VMEM((groups, length, 3 * HEAD), f32),
            pltpu.VMEM((groups, length, HEAD), bf16),
            pltpu.VMEM((groups, length, HEAD), bf16),
            pltpu.VMEM((groups, length, HEAD), bf16),
            pltpu.VMEM((groups, length, length), f32),
            pltpu.VMEM((groups, length, HEAD), bf16),
            pltpu.VMEM((groups, length, HEAD), bf16),
            pltpu.VMEM((groups, length, 3 * HEAD), bf16),
            pltpu.VMEM((CHUNKS, length, chunk), bf16),
            pltpu.VMEM((CHUNKS, length // 2, chunk), bf16),
            pltpu.VMEM((CHUNKS, length // 2, chunk), bf16),
            pltpu.VMEM((CHUNKS, ns // 2, rows, chunk), bf16),
            pltpu.VMEM((CHUNKS, length, chunk), bf16),
            pltpu.VMEM((CHUNKS, length // 2, chunk), bf16),
            pltpu.VMEM((CHUNKS, length // 2, chunk), bf16),
            pltpu.VMEM((CHUNKS, ns // 2, rows, chunk), bf16),
            dma((4,)),
            dma((rows // PIECE, ns)), dma((rows // PIECE, ns)),
            dma((rows // PIECE, ns)), dma((rows // PIECE, ns)),
            dma((nc,)), dma((nc,)), dma((nc,)), dma((nc,)),
            dma((nc,)), dma((nc,)), dma((ns,)), dma((ns,)),
            dma((CHUNKS,)), dma((CHUNKS,)), dma((CHUNKS, ns // 2)), dma((CHUNKS, ns // 2)),
            dma((CHUNKS,)), dma((CHUNKS,)), dma((CHUNKS, ns // 2)), dma((CHUNKS, ns // 2)),
        ],
        compiler_params=pltpu.CompilerParams(
            collective_id=0, has_side_effects=True, vmem_limit_bytes=66000000
        ),
    )(
        act_rows, cos_tab, sin_tab * sign_vec, mod_weight, latent[0], cotangent[0],
        input_weight.reshape(slab, groups * 3 * HEAD),
        output_weight.reshape(groups * HEAD, piece),
    )
    return (block_out[None], latent_grad[None])


def solution(mesh):
    placed = (
        P("cand", "seq", None),
        P(),
        P(),
        P("cand", "seq"),
        P("cand", "seq", None),
        P("seq", None, "cand"),
        P("cand", "seq", None),
    )
    return jax.shard_map(
        on_device,
        mesh=mesh,
        in_specs=placed,
        out_specs=(P("cand", "seq", None), P("cand", "seq", None)),
        check_vma=False,
    )
```

```python
import functools

import jax
import jax.numpy as jnp
import numpy as np
from jax import lax
from jax.experimental import pallas as pl
from jax.experimental.pallas import tpu as pltpu
from jax.sharding import PartitionSpec as P

HEAD = 128
CHUNKS = 4
PARTS = 1
MESH = pl.DeviceIdType.MESH


epsilon = 1e-06


def time_embed(timesteps, feature_width):
    half_size = feature_width // 2
    freq_rate = jnp.exp(-jnp.log(10000.0) * jnp.arange(half_size, dtype=jnp.float32) / half_size)
    angles = timesteps.astype(jnp.float32)[:, None] * freq_rate[None, :]
    return jnp.concatenate([jnp.cos(angles), jnp.sin(angles)], axis=1)


def rope_tables(positions, head_size):
    first_size = head_size // 8
    other_size = (head_size - first_size) // 2
    pieces = []
    swapped = []
    sign_vec = []
    offset = 0
    for axis_id, width_part in enumerate((first_size, other_size, other_size)):
        half_size = width_part // 2
        freq_rate = jnp.exp(
            -jnp.log(256.0) * 2.0 * jnp.arange(half_size, dtype=jnp.float32) / width_part
        )
        angle_part = positions[axis_id].astype(jnp.float32)[:, None] * freq_rate[None, :]
        pieces.append(angle_part)
        pieces.append(angle_part)
        swapped += list(range(offset + half_size, offset + width_part)) + list(
            range(offset, offset + half_size)
        )
        sign_vec += [-1.0] * half_size + [1.0] * half_size
        offset += width_part
    angles = jnp.concatenate(pieces, axis=1)
    return (
        jnp.cos(angles),
        jnp.sin(angles),
        np.array(swapped, np.int32),
        np.array(sign_vec, np.float32),
    )


def swap_pairs(values):
    lane = lax.broadcasted_iota(jnp.int32, values.shape, 1)
    small = HEAD // 8
    large = (HEAD - small) // 2
    near = jnp.where(
        lane < small // 2,
        pltpu.roll(values, HEAD - small // 2, 1),
        pltpu.roll(values, small // 2, 1),
    )
    upper = ((lane >= small) & (lane < small + large // 2)) | (
        (lane >= small + large) & (lane < small + large + large // 2)
    )
    far = jnp.where(
        upper, pltpu.roll(values, HEAD - large // 2, 1), pltpu.roll(values, large // 2, 1)
    )
    return jnp.where(lane < small, near, far)


def dot_nt(left, right):
    return lax.dot_general(left, right, (((1,), (1,)), ((), ())), preferred_element_type=jnp.float32)


def dot_tn(left, right):
    return lax.dot_general(left, right, (((0,), (0,)), ((), ())), preferred_element_type=jnp.float32)


def inverse_rms(values):
    return lax.rsqrt(jnp.mean(values * values, -1, keepdims=True) + epsilon)


def layer_norm(values):
    centred = values - jnp.mean(values, -1, keepdims=True)
    inverse_std = lax.rsqrt(jnp.mean(centred * centred, -1, keepdims=True) + epsilon)
    return (centred * inverse_std, inverse_std)


def step_kernel(
    nc, ns,
    act_ref, cos_ref, sin_ref, mod_w_ref, latent_ref, cot_ref, w_in_ref, w_out_ref,
    block_ref, grad_ref,
    part, part_in, mine, mod_all, vecs,
    lat_all, cot_all, w_in_all, w_out_all, x_all, proj, q_all, k_all, v_all, probs, att, d_att,
    d_proj, mix_out, mix_near, mix_sum, mix_in, dm_out, dm_near, dm_sum, dm_in,
    own_sem, lat_s, lat_r, cot_s, cot_r, wi_s, wi_r, wo_s, wo_r, m1_s, m1_r, m2_s, m2_r,
    mxn_s, mxn_r, mx_s, mx_r, dmn_s, dmn_r, dm_s, dm_r,
):
    me_c = lax.axis_index("cand")
    me_s = lax.axis_index("seq")
    rows, width = latent_ref.shape
    length = rows * ns
    slab = w_in_ref.shape[0]
    groups = q_all.shape[0]
    cols = mod_w_ref.shape[1]
    piece = w_out_ref.shape[1]
    chunk = width // CHUNKS
    half = nc // 2
    mate = me_c + 1 - 2 * lax.rem(me_c, 2)
    far = ns // 2
    me_y, me_z = lax.rem(me_s, 2), lax.div(me_s, 2)
    near = me_s + 1 - 2 * me_y
    score_scale = HEAD ** (-0.5)

    def seq_peer(k):
        return lax.rem(me_s + k, ns)

    def place(index):
        return lax.rem(index, 2) * far + lax.div(index, 2)

    def rows_of(index, size):
        return pl.ds(pl.multiple_of(index * size, size), size)

    def remote(src, dst, send, recv, cand, seq):
        copy = pltpu.make_async_remote_copy(
            src_ref=src, dst_ref=dst, send_sem=send, recv_sem=recv,
            device_id=(cand, seq), device_id_type=MESH,
        )
        copy.start()
        return copy

    barrier = pltpu.get_barrier_semaphore()
    for k in range(1, nc):
        pl.semaphore_signal(
            barrier, inc=1, device_id=(lax.rem(me_c + k, nc), me_s), device_id_type=MESH
        )
    for k in range(1, ns):
        pl.semaphore_signal(barrier, inc=1, device_id=(me_c, seq_peer(k)), device_id_type=MESH)

    own = [
        pltpu.make_async_copy(latent_ref, lat_all.at[rows_of(place(me_s), rows)], own_sem.at[0]),
        pltpu.make_async_copy(cot_ref, cot_all.at[rows_of(place(me_s), rows)], own_sem.at[1]),
        pltpu.make_async_copy(w_in_ref, w_in_all.at[rows_of(me_c, slab)], own_sem.at[2]),
        pltpu.make_async_copy(w_out_ref, w_out_all.at[me_c], own_sem.at[3]),
    ]
    for copy in own:
        copy.start()
    product = jnp.dot(act_ref[...], mod_w_ref[...], preferred_element_type=jnp.float32)
    for c in range(nc):
        part[c] = product[8 * c : 8 * c + 8]
    pl.semaphore_wait(barrier, nc - 1 + ns - 1)

    pieces = PARTS
    size = rows // PARTS

    def piece_of(whole, index, p):
        return whole.at[pl.ds(pl.multiple_of(place(index) * rows + p * size, size), size)]

    def seq_gather(src, whole, send, recv):
        near_copies, far_copies = [], []
        for p in range(pieces):
            from_here = src.at[pl.ds(p * size, size)]
            there = piece_of(whole, me_s, p)
            near_copies.append(
                remote(from_here, there, send.at[p, 0], recv.at[p, 0], me_c, near)
            )
            far_copies.append(
                [
                    remote(from_here, there, send.at[p, j], recv.at[p, j], me_c, seq_peer(2 * j))
                    for j in range(1, far)
                ]
            )
        return near_copies, far_copies

    def seq_forward(far_copies, whole, send, recv, p):
        second = []
        for j in range(1, far):
            far_copies[p][j - 1].wait_recv()
            held = piece_of(whole, seq_peer(ns - 2 * j), p)
            second.append(
                remote(held, held, send.at[p, far + j], recv.at[p, far + j], me_c, near)
            )
        return second

    lat_near, lat_far = seq_gather(latent_ref, lat_all, lat_s, lat_r)
    m1 = []
    for k in range(1, nc):
        peer = lax.rem(me_c + k, nc)
        m1.append(remote(part.at[peer], part_in.at[me_c], m1_s.at[k], m1_r.at[k], peer, me_s))

    def cand_gather(src, spot, send, recv):
        first = [remote(src, spot(me_c), send.at[0], recv.at[0], mate, me_s)]
        for j in range(1, half):
            peer = lax.rem(me_c + 2 * j, nc)
            first.append(remote(src, spot(me_c), send.at[j], recv.at[j], peer, me_s))
        return first

    def cand_forward(first, spot, send, recv):
        second = []
        for j in range(1, half):
            first[j].wait_recv()
            held = spot(lax.rem(me_c - 2 * j + nc, nc))
            second.append(remote(held, held, send.at[half + j], recv.at[half + j], mate, me_s))
        return second

    def in_place(index):
        return w_in_all.at[rows_of(index, slab)]

    def out_place(index):
        return w_out_all.at[index]

    w_in = cand_gather(w_in_ref, in_place, wi_s, wi_r)
    w_out = cand_gather(w_out_ref, out_place, wo_s, wo_r)

    for copy in m1:
        copy.wait_recv()
    total = part[me_c]
    for k in range(1, nc):
        total = total + part_in[lax.rem(me_c - k + nc, nc)]
    mine[...] = total
    mod_all[me_s] = total
    m2 = [
        remote(mine, mod_all.at[me_s], m2_s.at[k], m2_r.at[k], me_c, seq_peer(k))
        for k in range(1, ns)
    ]
    lat_second = []
    for p in range(pieces):
        lat_second += seq_forward(lat_far, lat_all, lat_s, lat_r, p)
    cot_near, cot_far = seq_gather(cot_ref, cot_all, cot_s, cot_r)
    cot_second = []
    for copy in lat_near + lat_second + m2:
        copy.wait_recv()
    own[0].wait()
    for s in range(ns):
        at = s * cols
        while at < (s + 1) * cols:
            kind = at // width
            stop = min((s + 1) * cols, (kind + 1) * width)
            vecs[kind, :, at - kind * width : stop - kind * width] = mod_all[
                s, :, at - s * cols : stop - s * cols
            ]
            at = stop

    def norm_rows(index, _):
        at = rows_of(index, 16)
        normed, _inverse = layer_norm(lat_all[at].astype(jnp.float32))
        x_all[at] = (normed * (1.0 + vecs[1, 0:1]) + vecs[0, 0:1]).astype(jnp.bfloat16)
        return 0

    lax.fori_loop(0, length // 16, norm_rows, 0)
    cot_second += seq_forward(cot_far, cot_all, cot_s, cot_r, 0)
    w_in_second = cand_forward(w_in, in_place, wi_s, wi_r)
    w_in[0].wait_recv()
    own[2].wait()
    for copy in w_in_second:
        copy.wait_recv()
    w_out_second = cand_forward(w_out, out_place, wo_s, wo_r)

    tile = 3 * HEAD

    def project(index, _):
        at = pl.ds(pl.multiple_of(index * tile, tile), tile)
        proj[index] = jnp.dot(x_all[...], w_in_all[:, at], preferred_element_type=jnp.float32)
        return 0

    lax.fori_loop(0, groups, project, 0)

    def head_forward(h, _):
        query = proj[h, :, 0:HEAD]
        key = proj[h, :, HEAD : 2 * HEAD]
        query_n = query * inverse_rms(query)
        key_n = key * inverse_rms(key)
        q_rot = (query_n * cos_ref[...] + swap_pairs(query_n) * sin_ref[...]).astype(jnp.bfloat16)
        k_rot = (key_n * cos_ref[...] + swap_pairs(key_n) * sin_ref[...]).astype(jnp.bfloat16)
        values = proj[h, :, 2 * HEAD :].astype(jnp.bfloat16)
        q_all[h] = q_rot
        k_all[h] = k_rot
        v_all[h] = values
        weights = jnp.exp(dot_nt(q_rot, k_rot) * score_scale - HEAD**0.5)
        share = weights * (1.0 / jnp.sum(weights, -1, keepdims=True))
        probs[h] = share
        att[h] = jnp.dot(
            share.astype(jnp.bfloat16), values, preferred_element_type=jnp.float32
        ).astype(jnp.bfloat16)
        return 0

    lax.fori_loop(0, groups, head_forward, 0)
    for p in range(1, pieces):
        cot_second += seq_forward(cot_far, cot_all, cot_s, cot_r, p)

    own[3].wait()
    w_out[0].wait_recv()
    for copy in w_out_second:
        copy.wait_recv()

    def scatter_near(out, into, send, recv, j):
        away = out.at[j, rows_of(1 - me_y, far * rows)]
        return remote(away, into.at[j], send.at[j], recv.at[j], me_c, near)

    def scatter_far(first, out, into, sums, landed, send, recv, j):
        first.wait_recv()
        here = out[j, rows_of(me_y, far * rows)].astype(jnp.float32)
        sums[j] = (here + into[j].astype(jnp.float32)).astype(jnp.bfloat16)
        copies = []
        for k in range(1, far):
            peer = lax.rem(me_z + k, far)
            copies.append(
                remote(
                    sums.at[j, rows_of(peer, rows)], landed.at[j, me_z],
                    send.at[j, k], recv.at[j, k], me_c, 2 * peer + me_y,
                )
            )
        return copies

    mixed_near = []
    span = max(chunk, piece)
    for n in range(width // span):
        for i in range(span // piece):
            c = n * (span // piece) + i
            block = jnp.zeros((length, piece), jnp.float32)
            for h in range(groups):
                block = block + jnp.dot(
                    att[h], w_out_all[c, h * HEAD : (h + 1) * HEAD], preferred_element_type=jnp.float32
                )
            block = block.astype(jnp.bfloat16)
            if piece < chunk:
                mix_out[n, :, i * piece : (i + 1) * piece] = block
            else:
                for m in range(span // chunk):
                    mix_out[n * (span // chunk) + m] = block[:, m * chunk : (m + 1) * chunk]
        for m in range(span // chunk):
            j = n * (span // chunk) + m
            mixed_near.append(scatter_near(mix_out, mix_near, mxn_s, mxn_r, j))

    for copy in cot_near + cot_second:
        copy.wait_recv()
    own[1].wait()

    def gate_rows(index, _):
        at = rows_of(index, 16)
        x_all[at] = (cot_all[at].astype(jnp.float32) * vecs[2, 0:1]).astype(jnp.bfloat16)
        return 0

    lax.fori_loop(0, length // 16, gate_rows, 0)
    for h in range(groups):
        block = jnp.zeros((length, HEAD), jnp.float32)
        for c in range(nc):
            block = block + dot_nt(
                x_all[:, c * piece : (c + 1) * piece], w_out_all[c, h * HEAD : (h + 1) * HEAD]
            )
        d_att[h] = block.astype(jnp.bfloat16)

    def back_norm(d_rot, raw):
        inverse = inverse_rms(raw)
        normed = raw * inverse
        d_normed = d_rot * cos_ref[...] - swap_pairs(d_rot) * sin_ref[...]
        return inverse * (d_normed - normed * jnp.mean(d_normed * normed, -1, keepdims=True))

    def head_backward(h, _):
        d_heads = d_att[h]
        share = probs[h]
        d_values = dot_tn(share.astype(jnp.bfloat16), d_heads)
        d_probs = dot_nt(d_heads, v_all[h])
        d_scores = (share * (d_probs - jnp.sum(share * d_probs, -1, keepdims=True))).astype(
            jnp.bfloat16
        )
        d_qrot = jnp.dot(d_scores, k_all[h], preferred_element_type=jnp.float32) * score_scale
        d_krot = dot_tn(d_scores, q_all[h]) * score_scale
        d_query = back_norm(d_qrot, proj[h, :, 0:HEAD])
        d_key = back_norm(d_krot, proj[h, :, HEAD : 2 * HEAD])
        d_proj[h, :, 0:HEAD] = d_query.astype(jnp.bfloat16)
        d_proj[h, :, HEAD : 2 * HEAD] = d_key.astype(jnp.bfloat16)
        d_proj[h, :, 2 * HEAD :] = d_values.astype(jnp.bfloat16)
        return 0

    lax.fori_loop(0, groups, head_backward, 0)

    d_near = []
    mixed = []
    for j in range(CHUNKS):
        block = jnp.zeros((length, chunk), jnp.float32)
        for h in range(groups):
            block = block + dot_nt(
                d_proj[h], w_in_all[j * chunk : (j + 1) * chunk, h * tile : (h + 1) * tile]
            )
        dm_out[j] = block.astype(jnp.bfloat16)
        d_near.append(scatter_near(dm_out, dm_near, dmn_s, dmn_r, j))
        mixed.append(
            scatter_far(mixed_near[j], mix_out, mix_near, mix_sum, mix_in, mx_s, mx_r, j)
        )
    d_mod = [
        scatter_far(d_near[j], dm_out, dm_near, dm_sum, dm_in, dm_s, dm_r, j)
        for j in range(CHUNKS)
    ]

    def summed(sums, landed, j, at):
        start = pl.multiple_of(me_z * rows, rows) + at
        result = sums[j, pl.ds(pl.multiple_of(start, 16), 16)].astype(jnp.float32)
        for k in range(1, far):
            result = result + landed[j, lax.rem(me_z + k, far), at : at + 16].astype(jnp.float32)
        return result

    for j in range(CHUNKS):
        for copy in mixed[j]:
            copy.wait_recv()
    for at in range(0, rows, 16):
        for j in range(CHUNKS):
            part_cols = slice(j * chunk, (j + 1) * chunk)
            own_rows = pl.ds(pl.multiple_of(place(me_s) * rows + at, 16), 16)
            block_ref[at : at + 16, part_cols] = (
                lat_all[own_rows, part_cols].astype(jnp.float32)
                + vecs[2, 0:1, part_cols] * summed(mix_sum, mix_in, j, at)
            ).astype(jnp.bfloat16)

    for j in range(CHUNKS):
        for copy in d_mod[j]:
            copy.wait_recv()
    for at in range(0, rows, 16):
        own_rows = pl.ds(pl.multiple_of(place(me_s) * rows + at, 16), 16)
        normed, inverse_std = layer_norm(lat_all[own_rows].astype(jnp.float32))
        d_normed = jnp.concatenate(
            [summed(dm_sum, dm_in, j, at) for j in range(CHUNKS)], axis=1
        ) * (1.0 + vecs[1, 0:1])
        grad_ref[at : at + 16] = cot_all[own_rows].astype(jnp.float32) + inverse_std * (
            d_normed
            - jnp.mean(d_normed, -1, keepdims=True)
            - normed * jnp.mean(d_normed * normed, -1, keepdims=True)
        )

    for copy in (
        lat_near + lat_second + sum(lat_far, []) + m1 + m2 + cot_near + cot_second
        + sum(cot_far, []) + w_in + w_out + w_in_second + w_out_second
        + mixed_near + d_near
    ):
        copy.wait_send()
    for j in range(CHUNKS):
        for copy in mixed[j] + d_mod[j]:
            copy.wait_send()


def on_device(latent, timesteps, positions, mod_weight, input_weight, output_weight, cotangent):
    nc = lax.axis_size("cand")
    ns = lax.axis_size("seq")
    rows, width = latent.shape[1:]
    length = rows * ns
    slab = input_weight.shape[0]
    groups = input_weight.shape[1]
    cols = mod_weight.shape[1]
    piece = output_weight.shape[2]
    chunk = width // CHUNKS
    time_act = jax.nn.silu(time_embed(timesteps, width)).astype(jnp.bfloat16)
    act_rows = lax.dynamic_slice_in_dim(time_act, lax.axis_index("cand") * slab, slab, 1)
    act_rows = jnp.repeat(act_rows, 8, axis=0)
    ordered = positions.reshape(-1, ns // 2, 2, rows).swapaxes(1, 2).reshape(-1, length)
    cos_tab, sin_tab, _swapped, sign_vec = rope_tables(ordered, HEAD)
    vmem = pl.BlockSpec(memory_space=pltpu.VMEM)
    anywhere = pl.BlockSpec(memory_space=pl.ANY)
    f32, bf16 = jnp.float32, jnp.bfloat16
    dma = pltpu.SemaphoreType.DMA
    block_out, latent_grad = pl.pallas_call(
        functools.partial(step_kernel, nc, ns),
        out_shape=(
            jax.ShapeDtypeStruct((rows, width), bf16),
            jax.ShapeDtypeStruct((rows, width), f32),
        ),
        in_specs=[vmem] * 4 + [anywhere] * 4,
        out_specs=(vmem, vmem),
        scratch_shapes=[
            pltpu.VMEM((nc, 8, cols), f32),
            pltpu.VMEM((nc, 8, cols), f32),
            pltpu.VMEM((8, cols), f32),
            pltpu.VMEM((ns, 8, cols), f32),
            pltpu.VMEM((3, 8, width), f32),
            pltpu.VMEM((length, width), bf16),
            pltpu.VMEM((length, width), bf16),
            pltpu.VMEM((slab * nc, groups * 3 * HEAD), bf16),
            pltpu.VMEM((nc, groups * HEAD, piece), bf16),
            pltpu.VMEM((length, width), bf16),
            pltpu.VMEM((groups, length, 3 * HEAD), f32),
            pltpu.VMEM((groups, length, HEAD), bf16),
            pltpu.VMEM((groups, length, HEAD), bf16),
            pltpu.VMEM((groups, length, HEAD), bf16),
            pltpu.VMEM((groups, length, length), f32),
            pltpu.VMEM((groups, length, HEAD), bf16),
            pltpu.VMEM((groups, length, HEAD), bf16),
            pltpu.VMEM((groups, length, 3 * HEAD), bf16),
            pltpu.VMEM((CHUNKS, length, chunk), bf16),
            pltpu.VMEM((CHUNKS, length // 2, chunk), bf16),
            pltpu.VMEM((CHUNKS, length // 2, chunk), bf16),
            pltpu.VMEM((CHUNKS, ns // 2, rows, chunk), bf16),
            pltpu.VMEM((CHUNKS, length, chunk), bf16),
            pltpu.VMEM((CHUNKS, length // 2, chunk), bf16),
            pltpu.VMEM((CHUNKS, length // 2, chunk), bf16),
            pltpu.VMEM((CHUNKS, ns // 2, rows, chunk), bf16),
            dma((4,)),
            dma((PARTS, ns)), dma((PARTS, ns)),
            dma((PARTS, ns)), dma((PARTS, ns)),
            dma((nc,)), dma((nc,)), dma((nc,)), dma((nc,)),
            dma((nc,)), dma((nc,)), dma((ns,)), dma((ns,)),
            dma((CHUNKS,)), dma((CHUNKS,)), dma((CHUNKS, ns // 2)), dma((CHUNKS, ns // 2)),
            dma((CHUNKS,)), dma((CHUNKS,)), dma((CHUNKS, ns // 2)), dma((CHUNKS, ns // 2)),
        ],
        compiler_params=pltpu.CompilerParams(
            collective_id=0, has_side_effects=True, vmem_limit_bytes=66000000
        ),
    )(
        act_rows, cos_tab, sin_tab * sign_vec, mod_weight, latent[0], cotangent[0],
        input_weight.reshape(slab, groups * 3 * HEAD),
        output_weight.reshape(groups * HEAD, piece),
    )
    return (block_out[None], latent_grad[None])


def solution(mesh):
    placed = (
        P("cand", "seq", None),
        P(),
        P(),
        P("cand", "seq"),
        P("cand", "seq", None),
        P("seq", None, "cand"),
        P("cand", "seq", None),
    )
    return jax.shard_map(
        on_device,
        mesh=mesh,
        in_specs=placed,
        out_specs=(P("cand", "seq", None), P("cand", "seq", None)),
        check_vma=False,
    )
```
